32 devices in a mesh: sym: 4 (over x, core), row: 8 (over z, y).
Axes of the slice: x: 2, y: 2, z: 4, core: 2. Of those that a mesh axis runs over, the one named last changes fastest.
Arguments:
- vectors: float32 [4, 32768, 256], P('sym', 'row'), may hold values from -6 to 6
- reflectors: float32 [4, 32768, 512], P('sym', 'row'), may hold values from -0.5 to 0.5
- factors: float32 [4, 4, 128, 128], P('sym'), may hold values from -0.03125 to 0.03125
- tiles: bfloat16 [4, 16, 512, 512], P('sym', 'row'), may hold values from -0.0029296875 to 0.0029296875
- tile_left: int32 [4, 16], P('sym', 'row'), may hold values from 0 to 7
- tile_right: int32 [4, 16], P('sym', 'row'), may hold values from 0 to 7
- tile_occupied_mask: int32 [4, 16], P('sym', 'row'), may hold values 0 or 1
- channels: int32 [4, 64], P('sym', 'row'), may hold values from 256 to 512
Outputs:
- dipole: float32 [4, 256, 256], P('sym', 'row')
The draws below stay inside these ranges and needn't reach their ends.
All inputs are finite; a program needn't handle non-finite values. No bound on the sum of `tile_occupied_mask` on one device may be relied on, other than what follows from the above.
Results may differ from the reference program's by a relative error of at most 0.0049.
Values may be sent and summed in bfloat16 or wider, within the bound.
A program may use at most 64 MiB of HBM per device.

```python
import jax
import jax.numpy as jnp
from jax import lax

EIG = 256
PANEL = 128
PANELS = 4
BLOCK = 512
TILE_SLOTS = 2
ORDER = 32768
SYMS = 4
BLOCKS_DEV = 8
BLOCKS = 64
TILES = 16


def set_ends(entries, rng, smallest, largest):
    extent = entries.shape
    place = [jax.random.randint(jax.random.fold_in(rng, axis), (), 0, extent[axis]) for axis in range(len(extent))]
    entries = entries.at[tuple(place)].set(smallest)
    longest = extent.index(max(extent))
    place[longest] = (place[longest] + 1) % extent[longest]
    return entries.at[tuple(place)].set(largest)


def levels(own_key, shape, shards, low, high):
    loudness = 1.0
    for dim, blocks in shards:
        heights = jax.random.uniform(jax.random.fold_in(jax.random.fold_in(own_key, 6), dim), (blocks,), jnp.float32, low / len(shards), high / len(shards))
        loudness = loudness * jnp.repeat(jnp.exp(heights), shape[dim] // blocks).reshape((-1,) + (1,) * (len(shape) - 1 - dim))
    return loudness


def bell_draw(rng, extent, scale, reach, cuts=(), held_as=jnp.bfloat16):
    drawn = scale * jax.random.normal(rng, extent, jnp.float32)
    if cuts:
        drawn = drawn * levels(rng, extent, cuts, -0.22, 0.18)
    return jnp.clip(drawn, -reach, reach).astype(held_as)


def setup_inputs(seed: int = 0) -> dict:
    key_of = jax.random.split(jax.random.key(seed), 9)
    vectors = bell_draw(key_of[0], (SYMS, ORDER, EIG), 1.0, 6.0, ((0, 4), (1, 8)), jnp.float32)
    reflectors = bell_draw(key_of[1], (SYMS, ORDER, PANELS * PANEL), PANEL ** -0.5, 0.5, ((0, 4), (1, 8)), jnp.float32)
    factors = bell_draw(key_of[2], (SYMS, PANELS, PANEL, PANEL), ORDER ** -0.5, 0.03125, ((0, 4),), jnp.float32)
    tiles = bell_draw(key_of[3], (SYMS, TILES, BLOCK, BLOCK), (BLOCK * BLOCK * TILES) ** -0.5, 0.0029296875, ((0, 4), (1, 8)))
    tile_left = set_ends(jax.random.randint(key_of[4], (SYMS, TILES), 0, BLOCKS_DEV), jax.random.fold_in(key_of[4], 1), 0, BLOCKS_DEV - 1).astype(jnp.int32)
    tile_right = set_ends(jax.random.randint(key_of[5], (SYMS, TILES), 0, BLOCKS_DEV), jax.random.fold_in(key_of[5], 1), 0, BLOCKS_DEV - 1).astype(jnp.int32)
    tile_occupied_mask = set_ends((jax.random.randint(key_of[6], (SYMS, TILES), 0, 4) < 3).astype(jnp.int32), jax.random.fold_in(key_of[6], 1), 0, 1)
    channels = set_ends(jax.random.randint(key_of[7], (SYMS, BLOCKS), BLOCK // 2, BLOCK + 1), jax.random.fold_in(key_of[7], 1), BLOCK // 2, BLOCK).astype(jnp.int32)
    return {"vectors": vectors, "reflectors": reflectors, "factors": factors, "tiles": tiles, "tile_left": tile_left, "tile_right": tile_right, "tile_occupied_mask": tile_occupied_mask, "channels": channels}


PRECISE = lax.Precision.HIGHEST


def back_transform(start, panels, factor_set):
    result = start
    for level in reversed(range(PANELS)):
        panel = panels[:, level * PANEL:(level + 1) * PANEL]
        inner_part = jnp.dot(panel.T, result, precision=PRECISE)
        result = result - jnp.dot(panel, jnp.dot(factor_set[level], inner_part, precision=PRECISE), precision=PRECISE)
    return result


def reference(vectors, reflectors, factors, tiles, tile_left, tile_right, tile_occupied_mask, channels):
    masked = []
    position = jnp.arange(BLOCK, dtype=jnp.int32)
    for symmetry_label in range(SYMS):
        result = back_transform(vectors[symmetry_label], reflectors[symmetry_label], factors[symmetry_label])
        keeper = (position[None, :] < channels[symmetry_label][:, None]).astype(jnp.float32)
        reshaped_block = result.reshape(BLOCKS, BLOCK, EIG) * keeper[:, :, None]
        masked.append(reshaped_block.astype(jnp.bfloat16))
    offsets = (jnp.arange(TILES, dtype=jnp.int32) // TILE_SLOTS) * BLOCKS_DEV
    dipole_output_list = []
    for symmetry_label in range(SYMS):
        paired_symmetry = (symmetry_label + 1) % SYMS
        bra_state_rows = masked[symmetry_label][(offsets + tile_left[symmetry_label]).astype(jnp.int32)]
        right_rows = masked[paired_symmetry][(offsets + tile_right[symmetry_label]).astype(jnp.int32)]
        bra_ket_product = jnp.einsum("tij,tjk->tik", tiles[symmetry_label].astype(jnp.float32), right_rows.astype(jnp.float32)).astype(jnp.bfloat16)
        tile_presence_mask = tile_occupied_mask[symmetry_label].astype(jnp.float32)
        dipole_output_list.append(jnp.einsum("agx,agh,a->xh", bra_state_rows.astype(jnp.float32), bra_ket_product.astype(jnp.float32), tile_presence_mask))
    return jnp.stack(dipole_output_list)
```

```python
import functools

import jax
import jax.numpy as jnp
from jax import lax
from jax.experimental import pallas as pl
from jax.experimental.pallas import tpu as pltpu
from jax.sharding import PartitionSpec as P

BLOCK = 512
LANES = 128
PACK = 16
TOP = 15.0
MARGIN = 1e-3
LEAST = 2.0**-100
MOST = 2.0**100
F32 = jnp.float32
BF16 = jnp.bfloat16
I16 = jnp.int16
MESH = pl.DeviceIdType.MESH


def split(value):
    high = value.astype(BF16)
    return high, (value - high.astype(F32)).astype(BF16)


def contract(first, second, dims):
    high, low = first
    other_high, other_low = second

    def dot(a, b):
        return lax.dot_general(a, b, (dims, ((), ())), preferred_element_type=F32)

    return dot(high, other_high) + (dot(high, other_low) + dot(low, other_high))


ROWS = ((0,), (0,))
PLAIN = ((1,), (0,))
COLUMNS = ((1,), (1,))


def coupled_ranges(first, count):
    if count < 2:
        return []
    half = count // 2
    here = [(first, half, first + half, count - half)]
    return here + coupled_ranges(first, half) + coupled_ranges(first + half, count - half)


def padded(rows):
    return -(-rows // PACK) * PACK


def encode(value, target):
    rows = value.shape[0]
    groups = value.reshape(rows // 8, 8, LANES)
    peak = jnp.clip(jnp.max(jnp.abs(groups), axis=0), LEAST, MOST)
    level = jnp.ceil(jnp.log2(peak) + MARGIN) - TOP
    codes = jnp.round(groups * jnp.exp2(-level)[None])
    target[:rows, :] = codes.reshape(rows, LANES).astype(jnp.int32).astype(I16)
    both = jnp.concatenate([level, level], axis=0)
    target[padded(rows) :, :] = both.astype(jnp.int32).astype(I16)


def decode(source, rows):
    level = source[padded(rows) :, :].astype(jnp.int32).astype(F32)[:8]
    groups = source[:rows, :].astype(jnp.int32).astype(F32).reshape(rows // 8, 8, LANES)
    return (groups * jnp.exp2(level)[None]).reshape(rows, LANES)


def kernel(
    n,
    syms,
    x_hbm,
    v_hbm,
    f_hbm,
    tiles_hbm,
    right_ref,
    left_ref,
    occupied_ref,
    channels_ref,
    out_ref,
    x_buf,
    v_buf,
    v_high,
    v_low,
    slots_vmem,
    slots_smem,
    coupled_part,
    coupled_out,
    coupled_in,
    coupled_all,
    coupled,
    inner_part,
    inner_out,
    inner_in,
    inner_all,
    t_ref,
    u_high,
    u_low,
    ket_out,
    ket_in,
    bras,
    own,
    dipole_out,
    dipole_in,
    f_ref,
    tiles_ref,
    x_sem,
    v_sem,
    slot_sem,
    operand_sem,
    coupled_send,
    coupled_recv,
    inner_send,
    inner_recv,
    ket_send,
    ket_recv,
    dipole_send,
    dipole_recv,
):
    panels, width, _ = f_ref.shape
    blocks, _, eig = x_buf.shape
    tile_slots = tiles_ref.shape[0]
    halves = eig // LANES
    sym = lax.axis_index("sym")
    me = lax.axis_index("row")
    after = lax.rem(sym + 1, syms)
    before = lax.rem(sym + syms - 1, syms)

    def load(source, target, sems, r):
        return pltpu.make_async_copy(source.at[r], target.at[r], sems.at[r])

    for r in range(blocks):
        load(v_hbm, v_buf, v_sem, r).start()
    for r in range(blocks):
        load(x_hbm, x_buf, x_sem, r).start()

    f_copy = pltpu.make_async_copy(f_hbm, f_ref, operand_sem.at[0])
    f_copy.start()
    tiles_copy = pltpu.make_async_copy(tiles_hbm, tiles_ref, operand_sem.at[1])
    tiles_copy.start()

    barrier = pltpu.get_barrier_semaphore()
    for d in range(1, n):
        pl.semaphore_signal(
            barrier, inc=1, device_id=(sym, lax.rem(me + d, n)), device_id_type=MESH
        )
    for other in (after, before):
        pl.semaphore_signal(barrier, inc=1, device_id=(other, me), device_id_type=MESH)

    ranges = coupled_ranges(0, panels)

    def couple(r, sums):
        load(v_hbm, v_buf, v_sem, r).wait()
        high, low = split(v_buf[r])
        v_high[r] = high
        v_low[r] = low
        out = []
        for total, (a, ca, b, cb) in zip(sums, ranges):
            pa = slice(a * width, (a + ca) * width)
            pb = slice(b * width, (b + cb) * width)
            out.append(
                total + contract((high[:, pa], low[:, pa]), (high[:, pb], low[:, pb]), ROWS)
            )
        return tuple(out)

    sums = lax.fori_loop(
        0, blocks, couple, tuple(jnp.zeros((ca * width, cb * width), F32) for _, ca, _, cb in ranges)
    )
    where = {}
    place = 0
    for total, (a, ca, b, cb) in zip(sums, ranges):
        for i in range(ca):
            for j in range(cb):
                where[(a + i, b + j)] = place
                coupled_part[place : place + width, :] = total[
                    i * width : (i + 1) * width, j * width : (j + 1) * width
                ]
                place = place + width

    def piece(part, owner, rows):
        return part[pl.ds(pl.multiple_of(owner * rows, 8), rows), :]

    def send(source, target, sends, recvs, d, peer):
        copy = pltpu.make_async_remote_copy(
            src_ref=source,
            dst_ref=target,
            send_sem=sends.at[d - 1],
            recv_sem=recvs.at[d - 1],
            device_id=(sym, peer),
            device_id_type=MESH,
        )
        copy.start()
        return copy

    def scatter(part, outgoing, landing, sends, recvs, rows):
        copies = []
        for d in range(1, n):
            peer = lax.rem(me + d, n)
            encode(piece(part, peer, rows), outgoing.at[d - 1])
            copies.append(send(outgoing.at[d - 1], landing.at[d - 1], sends, recvs, d, peer))
        return copies

    def gather(copies, part, landing, gathered, sends, recvs, rows):
        total = piece(part, me, rows)
        for d in range(1, n):
            copies[d - 1].wait()
            total = total + decode(landing.at[d - 1], rows)
        encode(total, gathered.at[me])
        return [
            send(gathered.at[me], gathered.at[me], sends, recvs, d, lax.rem(me + d, n))
            for d in range(1, n)
        ]

    pl.semaphore_wait(barrier, n + 1)
    coupled_rows = place // n
    coupled_copies = scatter(
        coupled_part, coupled_out, coupled_in, coupled_send.at[0], coupled_recv.at[0], coupled_rows
    )
    slots_copy = pltpu.make_async_remote_copy(
        src_ref=right_ref,
        dst_ref=slots_vmem,
        send_sem=slot_sem.at[0],
        recv_sem=slot_sem.at[1],
        device_id=(after, me),
        device_id_type=MESH,
    )
    slots_copy.start()

    def project(r, total):
        load(x_hbm, x_buf, x_sem, r).wait()
        return total + contract(split(x_buf[r]), (v_high[r], v_low[r]), ROWS)

    projected = lax.fori_loop(0, blocks, project, jnp.zeros((eig, panels * width), F32))
    inner_rows = panels * LANES // n
    inner_copies = []
    for h in range(halves):
        for k in range(panels):
            inner_part[h, k * LANES : (k + 1) * LANES, :] = projected[
                h * LANES : (h + 1) * LANES, k * width : (k + 1) * width
            ]
        inner_copies.append(
            scatter(
                inner_part.at[h],
                inner_out.at[h],
                inner_in.at[h],
                inner_send.at[0, h],
                inner_recv.at[0, h],
                inner_rows,
            )
        )
    coupled_copies = gather(
        coupled_copies,
        coupled_part,
        coupled_in,
        coupled_all,
        coupled_send.at[1],
        coupled_recv.at[1],
        coupled_rows,
    )

    slots_copy.wait()
    to_smem = pltpu.make_async_copy(slots_vmem, slots_smem, slot_sem.at[2])
    to_smem.start()

    def transfer_matrix():
        f_copy.wait()
        for k in reversed(range(panels)):
            here = slice(k * width, (k + 1) * width)
            t_ref[here, here] = f_ref[k]
            if k:
                t_ref[here, : k * width] = jnp.zeros((width, k * width), F32)
            if k < panels - 1:
                later = slice((k + 1) * width, panels * width)
                row = jnp.concatenate(
                    [coupled[where[(k, j)] : where[(k, j)] + width, :] for j in range(k + 1, panels)],
                    axis=1,
                )
                inner = contract(split(row), split(t_ref[later, later]), PLAIN)
                t_ref[here, later] = -contract(split(f_ref[k]), split(inner), PLAIN)

    def update(h):
        whole = jnp.concatenate([decode(inner_all.at[h, j], inner_rows) for j in range(n)], axis=0)
        gathered = jnp.concatenate(
            [whole[k * LANES : (k + 1) * LANES, :] for k in range(panels)], axis=1
        )
        high, low = split(contract(split(t_ref[...]), split(gathered), COLUMNS))
        u_high[h] = high
        u_low[h] = low

    def finished(slot, h):
        change = contract((v_high[slot], v_low[slot]), (u_high[h], u_low[h]), PLAIN)
        live = lax.broadcasted_iota(jnp.int32, (BLOCK, LANES), 0) < channels_ref[0, slot]
        value = x_buf[slot, :, h * LANES : (h + 1) * LANES] - change
        return jnp.where(live, value, 0.0)

    kets = {}

    def right_blocks(h):
        for t in range(tile_slots):
            ket_out[h, t] = finished(slots_smem[0, t], h).astype(BF16)
            copy = pltpu.make_async_remote_copy(
                src_ref=ket_out.at[h, t],
                dst_ref=ket_in.at[h, t],
                send_sem=ket_send.at[h, t],
                recv_sem=ket_recv.at[h, t],
                device_id=(before, me),
                device_id_type=MESH,
            )
            copy.start()
            kets[(h, t)] = copy

    def left_blocks(h):
        for t in range(tile_slots):
            occupied = occupied_ref[0, t].astype(F32)
            bras[t, :, h * LANES : (h + 1) * LANES] = (
                finished(left_ref[0, t], h) * occupied
            ).astype(BF16)

    for h in range(halves):
        inner_copies[h] = gather(
            inner_copies[h],
            inner_part.at[h],
            inner_in.at[h],
            inner_all.at[h],
            inner_send.at[1, h],
            inner_recv.at[1, h],
            inner_rows,
        )
    for copy in coupled_copies:
        copy.wait()
    for j in range(n):
        coupled[j * coupled_rows : (j + 1) * coupled_rows, :] = decode(coupled_all.at[j], coupled_rows)
    transfer_matrix()
    to_smem.wait()
    for h in range(halves):
        for copy in inner_copies[h]:
            copy.wait()
        update(h)
        right_blocks(h)
        left_blocks(h)

    share = eig // n
    tiles_copy.wait()
    sends = []
    for h in range(halves):
        total = jnp.zeros((eig, LANES), F32)
        for t in range(tile_slots):
            kets[(h, t)].wait()
            product = jnp.dot(tiles_ref[t], ket_in[h, t], preferred_element_type=F32).astype(BF16)
            total = total + lax.dot_general(
                bras[t], product, (ROWS, ((), ())), preferred_element_type=F32
            )
        own[h] = total.reshape(n, share, LANES)
        dipole_out[h] = total.reshape(n, share, LANES).astype(BF16)
        for d in range(1, n):
            target = lax.rem(me + d, n)
            copy = pltpu.make_async_remote_copy(
                src_ref=dipole_out.at[h, target],
                dst_ref=dipole_in.at[h, d - 1],
                send_sem=dipole_send.at[h, d - 1],
                recv_sem=dipole_recv.at[h, d - 1],
                device_id=(sym, target),
                device_id_type=MESH,
            )
            copy.start()
            sends.append((h, d, copy))
    results = [own[h, me] for h in range(halves)]
    for h, d, copy in sends:
        copy.wait()
        results[h] = results[h] + dipole_in[h, d - 1].astype(F32)
    for h in range(halves):
        out_ref[0, :, h * LANES : (h + 1) * LANES] = results[h]


def on_device(
    n,
    syms,
    vectors,
    reflectors,
    factors,
    tiles,
    tile_left,
    tile_right,
    tile_occupied_mask,
    channels,
):
    start = vectors[0]
    panels = reflectors[0]
    rows, eig = start.shape
    count, width, _ = factors.shape[1:]
    tile_slots = tiles.shape[1]
    halves = eig // LANES
    blocks = rows // BLOCK
    coupled = count * (count - 1) // 2 * width
    coupled_piece = padded(coupled // n) + PACK
    inner_piece = padded(count * LANES // n) + PACK
    share = eig // n
    dma = pltpu.SemaphoreType.DMA
    vmem = pl.BlockSpec(memory_space=pltpu.VMEM)
    smem = pl.BlockSpec(memory_space=pltpu.SMEM)
    hbm = pl.BlockSpec(memory_space=pl.ANY)
    return pl.pallas_call(
        functools.partial(kernel, n, syms),
        out_shape=jax.ShapeDtypeStruct((1, share, eig), F32),
        in_specs=[hbm, hbm, hbm, hbm, vmem, smem, smem, smem],
        out_specs=vmem,
        scratch_shapes=[
            pltpu.VMEM((blocks, BLOCK, eig), F32),
            pltpu.VMEM((blocks, BLOCK, count * width), F32),
            pltpu.VMEM((blocks, BLOCK, count * width), BF16),
            pltpu.VMEM((blocks, BLOCK, count * width), BF16),
            pltpu.VMEM((1, tile_slots), jnp.int32),
            pltpu.SMEM((1, tile_slots), jnp.int32),
            pltpu.VMEM((coupled, LANES), F32),
            pltpu.VMEM((n - 1, coupled_piece, LANES), I16),
            pltpu.VMEM((n - 1, coupled_piece, LANES), I16),
            pltpu.VMEM((n, coupled_piece, LANES), I16),
            pltpu.VMEM((coupled, LANES), F32),
            pltpu.VMEM((halves, count * LANES, LANES), F32),
            pltpu.VMEM((halves, n - 1, inner_piece, LANES), I16),
            pltpu.VMEM((halves, n - 1, inner_piece, LANES), I16),
            pltpu.VMEM((halves, n, inner_piece, LANES), I16),
            pltpu.VMEM((count * width, count * width), F32),
            pltpu.VMEM((halves, count * width, LANES), BF16),
            pltpu.VMEM((halves, count * width, LANES), BF16),
            pltpu.VMEM((halves, tile_slots, BLOCK, LANES), BF16),
            pltpu.VMEM((halves, tile_slots, BLOCK, LANES), BF16),
            pltpu.VMEM((tile_slots, BLOCK, eig), BF16),
            pltpu.VMEM((halves, n, share, LANES), F32),
            pltpu.VMEM((halves, n, share, LANES), BF16),
            pltpu.VMEM((halves, n - 1, share, LANES), BF16),
            pltpu.VMEM((count, width, width), F32),
            pltpu.VMEM((tile_slots, BLOCK, BLOCK), BF16),
            dma((blocks,)),
            dma((blocks,)),
            dma((3,)),
            dma((2,)),
            dma((2, n - 1)),
            dma((2, n - 1)),
            dma((2, halves, n - 1)),
            dma((2, halves, n - 1)),
            dma((halves, tile_slots)),
            dma((halves, tile_slots)),
            dma((halves, n - 1)),
            dma((halves, n - 1)),
        ],
        compiler_params=pltpu.CompilerParams(
            collective_id=0, has_side_effects=True, vmem_limit_bytes=60 * 1024 * 1024
        ),
    )(
        start.reshape(blocks, BLOCK, eig),
        panels.reshape(blocks, BLOCK, count * width),
        factors[0],
        tiles[0],
        tile_right,
        tile_left,
        tile_occupied_mask,
        channels,
    )


def solution(mesh):
    return jax.shard_map(
        functools.partial(on_device, mesh.shape["row"], mesh.shape["sym"]),
        mesh=mesh,
        in_specs=(
            P("sym", "row", None),
            P("sym", "row", None),
            P("sym", None, None, None),
            P("sym", "row", None, None),
            P("sym", "row"),
            P("sym", "row"),
            P("sym", "row"),
            P("sym", "row"),
        ),
        out_specs=P("sym", "row", None),
        check_vma=False,
    )
```

```python
import functools

import jax
import jax.numpy as jnp
from jax import lax
from jax.experimental import pallas as pl
from jax.experimental.pallas import tpu as pltpu
from jax.sharding import PartitionSpec as P

BLOCK = 512
LANES = 128
COUPLE_SPAN = 2
PROJECT_SPAN = 4
PACK = 16
TOP = 15.0
MARGIN = 1e-3
LEAST = 2.0**-100
MOST = 2.0**100
F32 = jnp.float32
BF16 = jnp.bfloat16
I16 = jnp.int16
MESH = pl.DeviceIdType.MESH


def split(value):
    high = value.astype(BF16)
    return high, (value - high.astype(F32)).astype(BF16)


def contract(first, second, dims):
    high, low = first
    other_high, other_low = second

    def dot(a, b):
        return lax.dot_general(a, b, (dims, ((), ())), preferred_element_type=F32)

    return dot(high, other_high) + (dot(high, other_low) + dot(low, other_high))


ROWS = ((0,), (0,))
PLAIN = ((1,), (0,))
COLUMNS = ((1,), (1,))


def couplings(panels):
    levels = []
    size = panels
    while size > 1:
        starts = range(0, panels, size)
        first = [a + i for a in starts for i in range(size // 2)]
        levels.append((first, [a + size // 2 for a in first], size // 2))
        size //= 2
    return levels


def padded(rows):
    return -(-rows // PACK) * PACK


def encode(value, target):
    rows = value.shape[0]
    groups = value.reshape(rows // 8, 8, LANES)
    peak = jnp.clip(jnp.max(jnp.abs(groups), axis=0), LEAST, MOST)
    level = jnp.ceil(jnp.log2(peak) + MARGIN) - TOP
    codes = jnp.round(groups * jnp.exp2(-level)[None])
    target[:rows, :] = codes.reshape(rows, LANES).astype(jnp.int32).astype(I16)
    both = jnp.concatenate([level, level], axis=0)
    target[padded(rows) :, :] = both.astype(jnp.int32).astype(I16)


def decode(source, rows):
    level = source[padded(rows) :, :].astype(jnp.int32).astype(F32)[:8]
    groups = source[:rows, :].astype(jnp.int32).astype(F32).reshape(rows // 8, 8, LANES)
    return (groups * jnp.exp2(level)[None]).reshape(rows, LANES)


def kernel(
    n,
    syms,
    x_hbm,
    v_hbm,
    f_hbm,
    tiles_hbm,
    right_ref,
    left_ref,
    occupied_ref,
    channels_ref,
    out_ref,
    x_buf,
    v_buf,
    v_high,
    v_low,
    slots_vmem,
    slots_smem,
    coupled_part,
    coupled_out,
    coupled_in,
    coupled_all,
    coupled,
    inner_part,
    inner_out,
    inner_in,
    inner_all,
    inner,
    x_turned,
    t_ref,
    u_high,
    u_low,
    ket_out,
    ket_in,
    bras,
    own,
    dipole_out,
    dipole_in,
    f_ref,
    tiles_ref,
    x_sem,
    v_sem,
    slot_sem,
    operand_sem,
    coupled_send,
    coupled_recv,
    inner_send,
    inner_recv,
    ket_send,
    ket_recv,
    dipole_send,
    dipole_recv,
):
    panels, width, _ = f_ref.shape
    blocks, _, eig = x_buf.shape
    tile_slots = tiles_ref.shape[0]
    halves = eig // LANES
    sym = lax.axis_index("sym")
    me = lax.axis_index("row")
    after = lax.rem(sym + 1, syms)
    before = lax.rem(sym + syms - 1, syms)

    def load(source, target, sems, r):
        return pltpu.make_async_copy(source.at[r], target.at[r], sems.at[r])

    for r in range(blocks):
        load(v_hbm, v_buf, v_sem, r).start()
    for r in range(blocks):
        load(x_hbm, x_buf, x_sem, r).start()

    f_copy = pltpu.make_async_copy(f_hbm, f_ref, operand_sem.at[0])
    f_copy.start()
    tiles_copy = pltpu.make_async_copy(tiles_hbm, tiles_ref, operand_sem.at[1])
    tiles_copy.start()

    barrier = pltpu.get_barrier_semaphore()
    for d in range(1, n):
        pl.semaphore_signal(
            barrier, inc=1, device_id=(sym, lax.rem(me + d, n)), device_id_type=MESH
        )
    for other in (after, before):
        pl.semaphore_signal(barrier, inc=1, device_id=(other, me), device_id_type=MESH)

    levels = couplings(panels)

    def side(both, chosen):
        return tuple(
            jnp.concatenate([half[:, k * width : (k + 1) * width] for k in chosen], axis=1)
            for half in both
        )

    def couple(r, sums):
        parts = []
        for i in range(COUPLE_SPAN):
            block = r * COUPLE_SPAN + i
            load(v_hbm, v_buf, v_sem, block).wait()
            both = split(v_buf[block])
            v_high[block], v_low[block] = both
            parts.append(both)
        both = tuple(jnp.concatenate(half, axis=0) for half in zip(*parts))
        return tuple(
            total + contract(side(both, first), side(both, second), ROWS)
            for total, (first, second, _) in zip(sums, levels)
        )

    half_width = panels // 2 * width
    sums = lax.fori_loop(
        0,
        blocks // COUPLE_SPAN,
        couple,
        tuple(jnp.zeros((half_width, half_width), F32) for _ in levels),
    )
    where = {}
    place = 0
    for total, (first, second, size) in zip(sums, levels):
        for i, a in enumerate(first):
            for j, b in enumerate(second):
                if i // size == j // size:
                    where[(a, b)] = place
                    coupled_part[place : place + width, :] = total[
                        i * width : (i + 1) * width, j * width : (j + 1) * width
                    ]
                    place = place + width

    def piece(part, owner, rows):
        return part[pl.ds(pl.multiple_of(owner * rows, 8), rows), :]

    def send(source, target, sends, recvs, d, peer):
        copy = pltpu.make_async_remote_copy(
            src_ref=source,
            dst_ref=target,
            send_sem=sends.at[d - 1],
            recv_sem=recvs.at[d - 1],
            device_id=(sym, peer),
            device_id_type=MESH,
        )
        copy.start()
        return copy

    def scatter(part, outgoing, landing, sends, recvs, rows):
        copies = []
        for d in range(1, n):
            peer = lax.rem(me + d, n)
            encode(piece(part, peer, rows), outgoing.at[d - 1])
            copies.append(send(outgoing.at[d - 1], landing.at[d - 1], sends, recvs, d, peer))
        return copies

    def collect(copies, part, landing, rows):
        total = piece(part, me, rows)
        for d in range(1, n):
            copies[d - 1].wait()
            total = total + decode(landing.at[d - 1], rows)
        return total

    def gather(total, gathered, sends, recvs):
        encode(total, gathered.at[me])
        return [
            send(gathered.at[me], gathered.at[me], sends, recvs, d, lax.rem(me + d, n))
            for d in range(1, n)
        ]

    pl.semaphore_wait(barrier, n + 1)
    coupled_rows = place // n
    coupled_copies = scatter(
        coupled_part, coupled_out, coupled_in, coupled_send.at[0], coupled_recv.at[0], coupled_rows
    )
    slots_copy = pltpu.make_async_remote_copy(
        src_ref=right_ref,
        dst_ref=slots_vmem,
        send_sem=slot_sem.at[0],
        recv_sem=slot_sem.at[1],
        device_id=(after, me),
        device_id_type=MESH,
    )
    slots_copy.start()

    share = LANES // n
    pairs = panels // 2
    inner_rows = halves * 2 * share
    inner_copies = []
    for q in range(pairs):
        columns = slice(2 * q * width, 2 * (q + 1) * width)

        def project(r, total):
            span = pl.ds(r * PROJECT_SPAN, PROJECT_SPAN)
            rows = PROJECT_SPAN * BLOCK
            if q == 0:
                for i in range(PROJECT_SPAN):
                    load(x_hbm, x_buf, x_sem, r * PROJECT_SPAN + i).wait()
                high, low = split(x_buf[span].reshape(rows, eig))
                x_turned[0, r] = high.T
                x_turned[1, r] = low.T
            high, low = x_turned[0, r], x_turned[1, r]
            both = (
                v_high[span, :, columns].reshape(rows, 2 * width),
                v_low[span, :, columns].reshape(rows, 2 * width),
            )
            return total + contract((high, low), both, PLAIN)

        projected = lax.fori_loop(
            0, blocks // PROJECT_SPAN, project, jnp.zeros((eig, 2 * width), F32)
        )
        for d in range(n):
            for h in range(halves):
                for k in range(2):
                    source = h * LANES + d * share
                    target = (d * halves + h) * 2 * share + k * share
                    inner_part[q, target : target + share, :] = projected[
                        source : source + share, k * width : (k + 1) * width
                    ]
        inner_copies.append(
            scatter(
                inner_part.at[q],
                inner_out.at[q],
                inner_in.at[q],
                inner_send.at[0, q],
                inner_recv.at[0, q],
                inner_rows,
            )
        )
    coupled_copies = gather(
        collect(coupled_copies, coupled_part, coupled_in, coupled_rows),
        coupled_all,
        coupled_send.at[1],
        coupled_recv.at[1],
    )

    slots_copy.wait()
    to_smem = pltpu.make_async_copy(slots_vmem, slots_smem, slot_sem.at[2])
    to_smem.start()

    def transfer_matrix():
        f_copy.wait()
        for k in reversed(range(panels)):
            here = slice(k * width, (k + 1) * width)
            t_ref[here, here] = f_ref[k]
            if k:
                t_ref[here, : k * width] = jnp.zeros((width, k * width), F32)
            if k < panels - 1:
                later = slice((k + 1) * width, panels * width)
                row = jnp.concatenate(
                    [coupled[where[(k, j)] : where[(k, j)] + width, :] for j in range(k + 1, panels)],
                    axis=1,
                )
                inner = contract(split(row), split(t_ref[later, later]), PLAIN)
                t_ref[here, later] = -contract(split(f_ref[k]), split(inner), PLAIN)

    def update(h):
        for j in range(n):
            value = decode(inner_all.at[h, j], panels * share)
            for k in range(panels):
                inner[h, j * share : (j + 1) * share, k * width : (k + 1) * width] = value[
                    k * share : (k + 1) * share, :
                ]
        high, low = split(contract(split(t_ref[...]), split(inner[h]), COLUMNS))
        u_high[:, h * LANES : (h + 1) * LANES] = high
        u_low[:, h * LANES : (h + 1) * LANES] = low

    def finished(slot, columns):
        change = contract(
            (v_high[slot], v_low[slot]), (u_high[:, columns], u_low[:, columns]), PLAIN
        )
        value = x_buf[slot, :, columns] - change
        live = lax.broadcasted_iota(jnp.int32, value.shape, 0) < channels_ref[0, slot]
        return jnp.where(live, value, 0.0)

    kets = {}

    def right_blocks(h):
        for t in range(tile_slots):
            ket_out[h, t] = finished(slots_smem[0, t], slice(h * LANES, (h + 1) * LANES)).astype(BF16)
            copy = pltpu.make_async_remote_copy(
                src_ref=ket_out.at[h, t],
                dst_ref=ket_in.at[h, t],
                send_sem=ket_send.at[h, t],
                recv_sem=ket_recv.at[h, t],
                device_id=(before, me),
                device_id_type=MESH,
            )
            copy.start()
            kets[(h, t)] = copy

    def left_blocks():
        for t in range(tile_slots):
            occupied = occupied_ref[0, t].astype(F32)
            bras[t] = (finished(left_ref[0, t], slice(0, eig)) * occupied).astype(BF16)

    totals = [
        collect(inner_copies[q], inner_part.at[q], inner_in.at[q], inner_rows) for q in range(pairs)
    ]
    inner_copies = [
        gather(
            jnp.concatenate(
                [total[h * 2 * share : (h + 1) * 2 * share, :] for total in totals], axis=0
            ),
            inner_all.at[h],
            inner_send.at[1, h],
            inner_recv.at[1, h],
        )
        for h in range(halves)
    ]
    for copy in coupled_copies:
        copy.wait()
    for j in range(n):
        coupled[j * coupled_rows : (j + 1) * coupled_rows, :] = decode(coupled_all.at[j], coupled_rows)
    transfer_matrix()
    to_smem.wait()
    for h in range(halves):
        for copy in inner_copies[h]:
            copy.wait()
        update(h)
        right_blocks(h)
    left_blocks()

    own_rows = eig // n
    tiles_copy.wait()
    sends = []
    for h in range(halves):
        total = jnp.zeros((eig, LANES), F32)
        for t in range(tile_slots):
            kets[(h, t)].wait()
            product = jnp.dot(tiles_ref[t], ket_in[h, t], preferred_element_type=F32).astype(BF16)
            total = total + lax.dot_general(
                bras[t], product, (ROWS, ((), ())), preferred_element_type=F32
            )
        own[h] = total.reshape(n, own_rows, LANES)
        dipole_out[h] = total.reshape(n, own_rows, LANES).astype(BF16)
        for d in range(1, n):
            target = lax.rem(me + d, n)
            copy = pltpu.make_async_remote_copy(
                src_ref=dipole_out.at[h, target],
                dst_ref=dipole_in.at[h, d - 1],
                send_sem=dipole_send.at[h, d - 1],
                recv_sem=dipole_recv.at[h, d - 1],
                device_id=(sym, target),
                device_id_type=MESH,
            )
            copy.start()
            sends.append((h, d, copy))
    results = [own[h, me] for h in range(halves)]
    for h, d, copy in sends:
        copy.wait()
        results[h] = results[h] + dipole_in[h, d - 1].astype(F32)
    for h in range(halves):
        out_ref[0, :, h * LANES : (h + 1) * LANES] = results[h]


def on_device(
    n,
    syms,
    vectors,
    reflectors,
    factors,
    tiles,
    tile_left,
    tile_right,
    tile_occupied_mask,
    channels,
):
    start = vectors[0]
    panels = reflectors[0]
    rows, eig = start.shape
    count, width, _ = factors.shape[1:]
    tile_slots = tiles.shape[1]
    halves = eig // LANES
    blocks = rows // BLOCK
    coupled = count * (count - 1) // 2 * width
    coupled_piece = padded(coupled // n) + PACK
    scatter_piece = padded(2 * eig // n) + PACK
    inner_piece = padded(count * LANES // n) + PACK
    spans = blocks // PROJECT_SPAN
    share = eig // n
    dma = pltpu.SemaphoreType.DMA
    vmem = pl.BlockSpec(memory_space=pltpu.VMEM)
    smem = pl.BlockSpec(memory_space=pltpu.SMEM)
    hbm = pl.BlockSpec(memory_space=pl.ANY)
    return pl.pallas_call(
        functools.partial(kernel, n, syms),
        out_shape=jax.ShapeDtypeStruct((1, share, eig), F32),
        in_specs=[hbm, hbm, hbm, hbm, vmem, smem, smem, smem],
        out_specs=vmem,
        scratch_shapes=[
            pltpu.VMEM((blocks, BLOCK, eig), F32),
            pltpu.VMEM((blocks, BLOCK, count * width), F32),
            pltpu.VMEM((blocks, BLOCK, count * width), BF16),
            pltpu.VMEM((blocks, BLOCK, count * width), BF16),
            pltpu.VMEM((1, tile_slots), jnp.int32),
            pltpu.SMEM((1, tile_slots), jnp.int32),
            pltpu.VMEM((coupled, LANES), F32),
            pltpu.VMEM((n - 1, coupled_piece, LANES), I16),
            pltpu.VMEM((n - 1, coupled_piece, LANES), I16),
            pltpu.VMEM((n, coupled_piece, LANES), I16),
            pltpu.VMEM((coupled, LANES), F32),
            pltpu.VMEM((count // 2, 2 * eig, LANES), F32),
            pltpu.VMEM((count // 2, n - 1, scatter_piece, LANES), I16),
            pltpu.VMEM((count // 2, n - 1, scatter_piece, LANES), I16),
            pltpu.VMEM((halves, n, inner_piece, LANES), I16),
            pltpu.VMEM((halves, LANES, count * width), F32),
            pltpu.VMEM((2, spans, eig, rows // spans), BF16),
            pltpu.VMEM((count * width, count * width), F32),
            pltpu.VMEM((count * width, eig), BF16),
            pltpu.VMEM((count * width, eig), BF16),
            pltpu.VMEM((halves, tile_slots, BLOCK, LANES), BF16),
            pltpu.VMEM((halves, tile_slots, BLOCK, LANES), BF16),
            pltpu.VMEM((tile_slots, BLOCK, eig), BF16),
            pltpu.VMEM((halves, n, share, LANES), F32),
            pltpu.VMEM((halves, n, share, LANES), BF16),
            pltpu.VMEM((halves, n - 1, share, LANES), BF16),
            pltpu.VMEM((count, width, width), F32),
            pltpu.VMEM((tile_slots, BLOCK, BLOCK), BF16),
            dma((blocks,)),
            dma((blocks,)),
            dma((3,)),
            dma((2,)),
            dma((2, n - 1)),
            dma((2, n - 1)),
            dma((2, max(halves, count // 2), n - 1)),
            dma((2, max(halves, count // 2), n - 1)),
            dma((halves, tile_slots)),
            dma((halves, tile_slots)),
            dma((halves, n - 1)),
            dma((halves, n - 1)),
        ],
        compiler_params=pltpu.CompilerParams(
            collective_id=0, has_side_effects=True, vmem_limit_bytes=60 * 1024 * 1024
        ),
    )(
        start.reshape(blocks, BLOCK, eig),
        panels.reshape(blocks, BLOCK, count * width),
        factors[0],
        tiles[0],
        tile_right,
        tile_left,
        tile_occupied_mask,
        channels,
    )


def solution(mesh):
    return jax.shard_map(
        functools.partial(on_device, mesh.shape["row"], mesh.shape["sym"]),
        mesh=mesh,
        in_specs=(
            P("sym", "row", None),
            P("sym", "row", None),
            P("sym", None, None, None),
            P("sym", "row", None, None),
            P("sym", "row"),
            P("sym", "row"),
            P("sym", "row"),
            P("sym", "row"),
        ),
        out_specs=P("sym", "row", None),
        check_vma=False,
    )
```

```python
import functools

import jax
import jax.numpy as jnp
from jax import lax
from jax.experimental import pallas as pl
from jax.experimental.pallas import tpu as pltpu
from jax.sharding import PartitionSpec as P

BLOCK = 512
LANES = 128
COUPLE_SPAN = 2
PROJECT_SPAN = 4
PACK = 16
TOP = 15.0
MARGIN = 1e-3
LEAST = 2.0**-100
MOST = 2.0**100
F32 = jnp.float32
BF16 = jnp.bfloat16
I16 = jnp.int16
MESH = pl.DeviceIdType.MESH


def split(value):
    high = value.astype(BF16)
    return high, (value - high.astype(F32)).astype(BF16)


def multiply(a, b, dims):
    return lax.dot_general(a, b, (dims, ((), ())), preferred_element_type=F32)


def contract(first, second, dims):
    high, low = first
    other_high, other_low = second
    crossed = multiply(high, other_low, dims) + multiply(low, other_high, dims)
    return multiply(high, other_high, dims) + crossed


ROWS = ((0,), (0,))
PLAIN = ((1,), (0,))
COLUMNS = ((1,), (1,))


def couplings(panels):
    levels = []
    size = panels
    while size > 1:
        starts = range(0, panels, size)
        first = [a + i for a in starts for i in range(size // 2)]
        levels.append((first, [a + size // 2 for a in first], size // 2))
        size //= 2
    return levels


def padded(rows):
    return -(-rows // PACK) * PACK


def encode(value, target):
    rows = value.shape[0]
    groups = value.reshape(rows // 8, 8, LANES)
    peak = jnp.clip(jnp.max(jnp.abs(groups), axis=0), LEAST, MOST)
    level = jnp.ceil(jnp.log2(peak) + MARGIN) - TOP
    codes = jnp.round(groups * jnp.exp2(-level)[None])
    target[:rows, :] = codes.reshape(rows, LANES).astype(jnp.int32).astype(I16)
    both = jnp.concatenate([level, level], axis=0)
    target[padded(rows) :, :] = both.astype(jnp.int32).astype(I16)


def decode(source, rows):
    level = source[padded(rows) :, :].astype(jnp.int32).astype(F32)[:8]
    groups = source[:rows, :].astype(jnp.int32).astype(F32).reshape(rows // 8, 8, LANES)
    return (groups * jnp.exp2(level)[None]).reshape(rows, LANES)


def kernel(
    n,
    syms,
    x_hbm,
    v_hbm,
    f_hbm,
    tiles_hbm,
    right_ref,
    left_ref,
    occupied_ref,
    channels_ref,
    out_ref,
    x_buf,
    v_buf,
    v_high,
    v_low,
    slots_vmem,
    slots_smem,
    coupled_part,
    coupled_out,
    coupled_in,
    coupled_all,
    coupled,
    inner_part,
    inner_out,
    inner_in,
    inner_all,
    inner,
    x_turned,
    t_ref,
    u_high,
    u_low,
    ket_out,
    ket_in,
    bras,
    own,
    dipole_out,
    dipole_in,
    f_ref,
    tiles_ref,
    x_sem,
    v_sem,
    slot_sem,
    operand_sem,
    coupled_send,
    coupled_recv,
    inner_send,
    inner_recv,
    ket_send,
    ket_recv,
    dipole_send,
    dipole_recv,
):
    panels, width, _ = f_ref.shape
    blocks, _, eig = x_buf.shape
    tile_slots = tiles_ref.shape[0]
    halves = eig // LANES
    sym = lax.axis_index("sym")
    me = lax.axis_index("row")
    after = lax.rem(sym + 1, syms)
    before = lax.rem(sym + syms - 1, syms)

    def load(source, target, sems, r):
        return pltpu.make_async_copy(source.at[r], target.at[r], sems.at[r])

    for r in range(blocks):
        load(v_hbm, v_buf, v_sem, r).start()
    for r in range(blocks):
        load(x_hbm, x_buf, x_sem, r).start()

    f_copy = pltpu.make_async_copy(f_hbm, f_ref, operand_sem.at[0])
    f_copy.start()
    tiles_copy = pltpu.make_async_copy(tiles_hbm, tiles_ref, operand_sem.at[1])
    tiles_copy.start()

    barrier = pltpu.get_barrier_semaphore()
    for d in range(1, n):
        pl.semaphore_signal(
            barrier, inc=1, device_id=(sym, lax.rem(me + d, n)), device_id_type=MESH
        )
    for other in (after, before):
        pl.semaphore_signal(barrier, inc=1, device_id=(other, me), device_id_type=MESH)

    levels = couplings(panels)

    def side(ref, span, chosen):
        rows = ref[span].reshape(COUPLE_SPAN * BLOCK, panels * width)
        return jnp.concatenate([rows[:, k * width : (k + 1) * width] for k in chosen], axis=1)

    def couple(r, sums):
        for i in range(COUPLE_SPAN):
            block = r * COUPLE_SPAN + i
            load(v_hbm, v_buf, v_sem, block).wait()
            v_high[block], v_low[block] = split(v_buf[block])
        span = pl.ds(r * COUPLE_SPAN, COUPLE_SPAN)
        return tuple(
            total
            + contract(
                (side(v_high, span, first), side(v_low, span, first)),
                (side(v_high, span, second), side(v_low, span, second)),
                ROWS,
            )
            for total, (first, second, _) in zip(sums, levels)
        )

    half_width = panels // 2 * width
    sums = lax.fori_loop(
        0,
        blocks // COUPLE_SPAN,
        couple,
        tuple(jnp.zeros((half_width, half_width), F32) for _ in levels),
    )
    where = {}
    blocks_of = [
        (total, first[i], second[j], i, j, i // size == j // size)
        for total, (first, second, size) in zip(sums, levels)
        for i in range(len(first))
        for j in range(len(second))
    ]
    place = 0
    for total, a, b, i, j, needed in sorted(blocks_of, key=lambda entry: not entry[-1]):
        coupled_part[place : place + width, :] = total[
            i * width : (i + 1) * width, j * width : (j + 1) * width
        ]
        if needed:
            where[(a, b)] = place
        place = place + width

    def piece(part, owner, rows):
        return part[pl.ds(pl.multiple_of(owner * rows, 8), rows), :]

    def send(source, target, sends, recvs, d, peer):
        copy = pltpu.make_async_remote_copy(
            src_ref=source,
            dst_ref=target,
            send_sem=sends.at[d - 1],
            recv_sem=recvs.at[d - 1],
            device_id=(sym, peer),
            device_id_type=MESH,
        )
        copy.start()
        return copy

    def scatter(part, outgoing, landing, sends, recvs, rows):
        copies = []
        for d in range(1, n):
            peer = lax.rem(me + d, n)
            encode(piece(part, peer, rows), outgoing.at[d - 1])
            copies.append(send(outgoing.at[d - 1], landing.at[d - 1], sends, recvs, d, peer))
        return copies

    def collect(copies, part, landing, rows):
        total = piece(part, me, rows)
        for d in range(1, n):
            copies[d - 1].wait()
            total = total + decode(landing.at[d - 1], rows)
        return total

    def gather(total, gathered, sends, recvs):
        encode(total, gathered.at[me])
        return [
            send(gathered.at[me], gathered.at[me], sends, recvs, d, lax.rem(me + d, n))
            for d in range(1, n)
        ]

    pl.semaphore_wait(barrier, n + 1)
    coupled_rows = len(where) * width // n
    coupled_copies = scatter(
        coupled_part, coupled_out, coupled_in, coupled_send.at[0], coupled_recv.at[0], coupled_rows
    )
    slots_copy = pltpu.make_async_remote_copy(
        src_ref=right_ref,
        dst_ref=slots_vmem,
        send_sem=slot_sem.at[0],
        recv_sem=slot_sem.at[1],
        device_id=(after, me),
        device_id_type=MESH,
    )
    slots_copy.start()

    share = LANES // n
    pairs = panels // 2
    inner_rows = halves * 2 * share
    inner_copies = []
    for q in range(pairs):
        columns = slice(2 * q * width, 2 * (q + 1) * width)

        def project(r, total):
            span = pl.ds(r * PROJECT_SPAN, PROJECT_SPAN)
            rows = PROJECT_SPAN * BLOCK
            both = (
                v_high[span, :, columns].reshape(rows, 2 * width),
                v_low[span, :, columns].reshape(rows, 2 * width),
            )
            if q == 0:
                for i in range(PROJECT_SPAN):
                    load(x_hbm, x_buf, x_sem, r * PROJECT_SPAN + i).wait()
                high, low = split(x_buf[span].reshape(rows, eig))
                x_turned[r, :eig, :] = high.T
                x_turned[r, eig:, :] = low.T
                turned = (x_turned[r, :eig, :], x_turned[r, eig:, :])
                return total + contract(turned, both, PLAIN)
            fine = multiply(x_turned[r], both[0], PLAIN)
            crossed = multiply(x_turned[r, :eig, :], both[1], PLAIN)
            return total + (fine[:eig] + (fine[eig:] + crossed))

        projected = lax.fori_loop(
            0, blocks // PROJECT_SPAN, project, jnp.zeros((eig, 2 * width), F32)
        )
        for d in range(n):
            for h in range(halves):
                for k in range(2):
                    source = h * LANES + d * share
                    target = (d * halves + h) * 2 * share + k * share
                    inner_part[q, target : target + share, :] = projected[
                        source : source + share, k * width : (k + 1) * width
                    ]
        inner_copies.append(
            scatter(
                inner_part.at[q],
                inner_out.at[q],
                inner_in.at[q],
                inner_send.at[0, q],
                inner_recv.at[0, q],
                inner_rows,
            )
        )
    coupled_copies = gather(
        collect(coupled_copies, coupled_part, coupled_in, coupled_rows),
        coupled_all,
        coupled_send.at[1],
        coupled_recv.at[1],
    )

    slots_copy.wait()
    to_smem = pltpu.make_async_copy(slots_vmem, slots_smem, slot_sem.at[2])
    to_smem.start()

    def transfer_matrix():
        f_copy.wait()
        for k in reversed(range(panels)):
            here = slice(k * width, (k + 1) * width)
            t_ref[here, here] = f_ref[k]
            if k:
                t_ref[here, : k * width] = jnp.zeros((width, k * width), F32)
            if k < panels - 1:
                later = slice((k + 1) * width, panels * width)
                row = jnp.concatenate(
                    [coupled[where[(k, j)] : where[(k, j)] + width, :] for j in range(k + 1, panels)],
                    axis=1,
                )
                inner = contract(split(row), split(t_ref[later, later]), PLAIN)
                t_ref[here, later] = -contract(split(f_ref[k]), split(inner), PLAIN)

    def update(h):
        for j in range(n):
            value = decode(inner_all.at[h, j], panels * share)
            for k in range(panels):
                inner[h, j * share : (j + 1) * share, k * width : (k + 1) * width] = value[
                    k * share : (k + 1) * share, :
                ]
        high, low = split(contract(split(t_ref[...]), split(inner[h]), COLUMNS))
        u_high[:, h * LANES : (h + 1) * LANES] = high
        u_low[:, h * LANES : (h + 1) * LANES] = low

    def finished(slot, columns):
        change = contract(
            (v_high[slot], v_low[slot]), (u_high[:, columns], u_low[:, columns]), PLAIN
        )
        value = x_buf[slot, :, columns] - change
        live = lax.broadcasted_iota(jnp.int32, value.shape, 0) < channels_ref[0, slot]
        return jnp.where(live, value, 0.0)

    kets = {}

    def right_blocks(h):
        for t in range(tile_slots):
            ket_out[h, t] = finished(slots_smem[0, t], slice(h * LANES, (h + 1) * LANES)).astype(BF16)
            copy = pltpu.make_async_remote_copy(
                src_ref=ket_out.at[h, t],
                dst_ref=ket_in.at[h, t],
                send_sem=ket_send.at[h, t],
                recv_sem=ket_recv.at[h, t],
                device_id=(before, me),
                device_id_type=MESH,
            )
            copy.start()
            kets[(h, t)] = copy

    def left_blocks():
        for t in range(tile_slots):
            occupied = occupied_ref[0, t].astype(F32)
            bras[t] = (finished(left_ref[0, t], slice(0, eig)) * occupied).astype(BF16)

    totals = [
        collect(inner_copies[q], inner_part.at[q], inner_in.at[q], inner_rows) for q in range(pairs)
    ]
    inner_copies = [
        gather(
            jnp.concatenate(
                [total[h * 2 * share : (h + 1) * 2 * share, :] for total in totals], axis=0
            ),
            inner_all.at[h],
            inner_send.at[1, h],
            inner_recv.at[1, h],
        )
        for h in range(halves)
    ]
    for copy in coupled_copies:
        copy.wait()
    for j in range(n):
        coupled[j * coupled_rows : (j + 1) * coupled_rows, :] = decode(coupled_all.at[j], coupled_rows)
    transfer_matrix()
    to_smem.wait()
    for h in range(halves):
        for copy in inner_copies[h]:
            copy.wait()
        update(h)
        right_blocks(h)
    left_blocks()

    own_rows = eig // n
    tiles_copy.wait()
    sends = []
    for h in range(halves):
        total = jnp.zeros((eig, LANES), F32)
        for t in range(tile_slots):
            kets[(h, t)].wait()
            product = jnp.dot(tiles_ref[t], ket_in[h, t], preferred_element_type=F32).astype(BF16)
            total = total + lax.dot_general(
                bras[t], product, (ROWS, ((), ())), preferred_element_type=F32
            )
        own[h] = total.reshape(n, own_rows, LANES)
        dipole_out[h] = total.reshape(n, own_rows, LANES).astype(BF16)
        for d in range(1, n):
            target = lax.rem(me + d, n)
            copy = pltpu.make_async_remote_copy(
                src_ref=dipole_out.at[h, target],
                dst_ref=dipole_in.at[h, d - 1],
                send_sem=dipole_send.at[h, d - 1],
                recv_sem=dipole_recv.at[h, d - 1],
                device_id=(sym, target),
                device_id_type=MESH,
            )
            copy.start()
            sends.append((h, d, copy))
    results = [own[h, me] for h in range(halves)]
    for h, d, copy in sends:
        copy.wait()
        results[h] = results[h] + dipole_in[h, d - 1].astype(F32)
    for h in range(halves):
        out_ref[0, :, h * LANES : (h + 1) * LANES] = results[h]


def on_device(
    n,
    syms,
    vectors,
    reflectors,
    factors,
    tiles,
    tile_left,
    tile_right,
    tile_occupied_mask,
    channels,
):
    start = vectors[0]
    panels = reflectors[0]
    rows, eig = start.shape
    count, width, _ = factors.shape[1:]
    tile_slots = tiles.shape[1]
    halves = eig // LANES
    blocks = rows // BLOCK
    coupled = count * (count - 1) // 2 * width
    coupled_piece = padded(coupled // n) + PACK
    products = len(couplings(count)) * (count // 2) ** 2 * width
    scatter_piece = padded(2 * eig // n) + PACK
    inner_piece = padded(count * LANES // n) + PACK
    spans = blocks // PROJECT_SPAN
    share = eig // n
    dma = pltpu.SemaphoreType.DMA
    vmem = pl.BlockSpec(memory_space=pltpu.VMEM)
    smem = pl.BlockSpec(memory_space=pltpu.SMEM)
    hbm = pl.BlockSpec(memory_space=pl.ANY)
    return pl.pallas_call(
        functools.partial(kernel, n, syms),
        out_shape=jax.ShapeDtypeStruct((1, share, eig), F32),
        in_specs=[hbm, hbm, hbm, hbm, vmem, smem, smem, smem],
        out_specs=vmem,
        scratch_shapes=[
            pltpu.VMEM((blocks, BLOCK, eig), F32),
            pltpu.VMEM((blocks, BLOCK, count * width), F32),
            pltpu.VMEM((blocks, BLOCK, count * width), BF16),
            pltpu.VMEM((blocks, BLOCK, count * width), BF16),
            pltpu.VMEM((1, tile_slots), jnp.int32),
            pltpu.SMEM((1, tile_slots), jnp.int32),
            pltpu.VMEM((products, LANES), F32),
            pltpu.VMEM((n - 1, coupled_piece, LANES), I16),
            pltpu.VMEM((n - 1, coupled_piece, LANES), I16),
            pltpu.VMEM((n, coupled_piece, LANES), I16),
            pltpu.VMEM((coupled, LANES), F32),
            pltpu.VMEM((count // 2, 2 * eig, LANES), F32),
            pltpu.VMEM((count // 2, n - 1, scatter_piece, LANES), I16),
            pltpu.VMEM((count // 2, n - 1, scatter_piece, LANES), I16),
            pltpu.VMEM((halves, n, inner_piece, LANES), I16),
            pltpu.VMEM((halves, LANES, count * width), F32),
            pltpu.VMEM((spans, 2 * eig, rows // spans), BF16),
            pltpu.VMEM((count * width, count * width), F32),
            pltpu.VMEM((count * width, eig), BF16),
            pltpu.VMEM((count * width, eig), BF16),
            pltpu.VMEM((halves, tile_slots, BLOCK, LANES), BF16),
            pltpu.VMEM((halves, tile_slots, BLOCK, LANES), BF16),
            pltpu.VMEM((tile_slots, BLOCK, eig), BF16),
            pltpu.VMEM((halves, n, share, LANES), F32),
            pltpu.VMEM((halves, n, share, LANES), BF16),
            pltpu.VMEM((halves, n - 1, share, LANES), BF16),
            pltpu.VMEM((count, width, width), F32),
            pltpu.VMEM((tile_slots, BLOCK, BLOCK), BF16),
            dma((blocks,)),
            dma((blocks,)),
            dma((3,)),
            dma((2,)),
            dma((2, n - 1)),
            dma((2, n - 1)),
            dma((2, max(halves, count // 2), n - 1)),
            dma((2, max(halves, count // 2), n - 1)),
            dma((halves, tile_slots)),
            dma((halves, tile_slots)),
            dma((halves, n - 1)),
            dma((halves, n - 1)),
        ],
        compiler_params=pltpu.CompilerParams(
            collective_id=0, has_side_effects=True, vmem_limit_bytes=60 * 1024 * 1024
        ),
    )(
        start.reshape(blocks, BLOCK, eig),
        panels.reshape(blocks, BLOCK, count * width),
        factors[0],
        tiles[0],
        tile_right,
        tile_left,
        tile_occupied_mask,
        channels,
    )


def solution(mesh):
    return jax.shard_map(
        functools.partial(on_device, mesh.shape["row"], mesh.shape["sym"]),
        mesh=mesh,
        in_specs=(
            P("sym", "row", None),
            P("sym", "row", None),
            P("sym", None, None, None),
            P("sym", "row", None, None),
            P("sym", "row"),
            P("sym", "row"),
            P("sym", "row"),
            P("sym", "row"),
        ),
        out_specs=P("sym", "row", None),
        check_vma=False,
    )
```

```python
import functools

import jax
import jax.numpy as jnp
from jax import lax
from jax.experimental import pallas as pl
from jax.experimental.pallas import tpu as pltpu
from jax.sharding import PartitionSpec as P

BLOCK = 512
LANES = 128
COUPLE_SPAN = 2
PROJECT_SPAN = 4
RING = 4
PAIR = 2
PACK = 16
TOP = 15.0
MARGIN = 1e-3
LEAST = 2.0**-100
MOST = 2.0**100
F32 = jnp.float32
BF16 = jnp.bfloat16
I16 = jnp.int16
MESH = pl.DeviceIdType.MESH


def split(value):
    high = value.astype(BF16)
    return high, (value - high.astype(F32)).astype(BF16)


def multiply(a, b, dims):
    return lax.dot_general(a, b, (dims, ((), ())), preferred_element_type=F32)


def contract(first, second, dims):
    high, low = first
    other_high, other_low = second
    crossed = multiply(high, other_low, dims) + multiply(low, other_high, dims)
    return multiply(high, other_high, dims) + crossed


ROWS = ((0,), (0,))
PLAIN = ((1,), (0,))
COLUMNS = ((1,), (1,))


def couplings(panels):
    levels = []
    size = panels
    while size > 1:
        starts = range(0, panels, size)
        first = [a + i for a in starts for i in range(size // 2)]
        levels.append((first, [a + size // 2 for a in first], size // 2))
        size //= 2
    return levels


def padded(rows):
    return -(-rows // PACK) * PACK


def encode(value, target):
    rows = value.shape[0]
    groups = value.reshape(rows // 8, 8, LANES)
    peak = jnp.clip(jnp.max(jnp.abs(groups), axis=0), LEAST, MOST)
    level = jnp.ceil(jnp.log2(peak) + MARGIN) - TOP
    codes = jnp.round(groups * jnp.exp2(-level)[None])
    target[:rows, :] = codes.reshape(rows, LANES).astype(jnp.int32).astype(I16)
    both = jnp.concatenate([level, level], axis=0)
    target[padded(rows) :, :] = both.astype(jnp.int32).astype(I16)


def decode(source, rows):
    level = source[padded(rows) :, :].astype(jnp.int32).astype(F32)[:8]
    groups = source[:rows, :].astype(jnp.int32).astype(F32).reshape(rows // 8, 8, LANES)
    return (groups * jnp.exp2(level)[None]).reshape(rows, LANES)


def kernel(
    n,
    syms,
    x_hbm,
    v_hbm,
    f_hbm,
    tiles_hbm,
    right_ref,
    left_ref,
    occupied_ref,
    channels_ref,
    out_ref,
    x_buf,
    v_buf,
    v_high,
    v_low,
    slots_vmem,
    slots_smem,
    coupled_part,
    coupled_out,
    coupled_in,
    coupled_pass,
    coupled_all,
    coupled,
    inner_part,
    inner_out,
    inner_in,
    inner_pass,
    inner_all,
    inner,
    x_turned,
    t_ref,
    u_high,
    u_low,
    ket_out,
    ket_in,
    bras,
    own,
    dipole_out,
    dipole_in,
    f_ref,
    tiles_ref,
    x_sem,
    v_sem,
    slot_sem,
    operand_sem,
    coupled_send,
    coupled_recv,
    inner_send,
    inner_recv,
    ket_send,
    ket_recv,
    dipole_send,
    dipole_recv,
):
    panels, width, _ = f_ref.shape
    blocks, _, eig = x_buf.shape
    tile_slots = tiles_ref.shape[0]
    halves = eig // LANES
    sym = lax.axis_index("sym")
    me = lax.axis_index("row")
    after = lax.rem(sym + 1, syms)
    before = lax.rem(sym + syms - 1, syms)

    def load(source, target, sems, r):
        return pltpu.make_async_copy(source.at[r], target.at[r], sems.at[r])

    for r in range(blocks):
        load(v_hbm, v_buf, v_sem, r).start()
    for r in range(blocks):
        load(x_hbm, x_buf, x_sem, r).start()

    f_copy = pltpu.make_async_copy(f_hbm, f_ref, operand_sem.at[0])
    f_copy.start()
    tiles_copy = pltpu.make_async_copy(tiles_hbm, tiles_ref, operand_sem.at[1])
    tiles_copy.start()

    barrier = pltpu.get_barrier_semaphore()
    for d in range(1, n):
        pl.semaphore_signal(
            barrier, inc=1, device_id=(sym, lax.rem(me + d, n)), device_id_type=MESH
        )
    for other in (after, before):
        pl.semaphore_signal(barrier, inc=1, device_id=(other, me), device_id_type=MESH)

    levels = couplings(panels)

    def side(ref, span, chosen):
        rows = ref[span].reshape(COUPLE_SPAN * BLOCK, panels * width)
        return jnp.concatenate([rows[:, k * width : (k + 1) * width] for k in chosen], axis=1)

    def couple(r, sums):
        for i in range(COUPLE_SPAN):
            block = r * COUPLE_SPAN + i
            load(v_hbm, v_buf, v_sem, block).wait()
            v_high[block], v_low[block] = split(v_buf[block])
        span = pl.ds(r * COUPLE_SPAN, COUPLE_SPAN)
        return tuple(
            total
            + contract(
                (side(v_high, span, first), side(v_low, span, first)),
                (side(v_high, span, second), side(v_low, span, second)),
                ROWS,
            )
            for total, (first, second, _) in zip(sums, levels)
        )

    half_width = panels // 2 * width
    sums = lax.fori_loop(
        0,
        blocks // COUPLE_SPAN,
        couple,
        tuple(jnp.zeros((half_width, half_width), F32) for _ in levels),
    )
    where = {}
    blocks_of = [
        (total, first[i], second[j], i, j, i // size == j // size)
        for total, (first, second, size) in zip(sums, levels)
        for i in range(len(first))
        for j in range(len(second))
    ]
    place = 0
    for total, a, b, i, j, needed in sorted(blocks_of, key=lambda entry: not entry[-1]):
        coupled_part[place : place + width, :] = total[
            i * width : (i + 1) * width, j * width : (j + 1) * width
        ]
        if needed:
            where[(a, b)] = place
        place = place + width

    def piece(part, owner, rows):
        return part[pl.ds(pl.multiple_of(owner * rows, 8), rows), :]

    def send(source, target, sems, k, peer):
        copy = pltpu.make_async_remote_copy(
            src_ref=source,
            dst_ref=target,
            send_sem=sems[0].at[k],
            recv_sem=sems[1].at[k],
            device_id=(sym, peer),
            device_id_type=MESH,
        )
        copy.start()
        return copy

    relayed = n == RING * PAIR
    if relayed:
        steps = [(a, b) for a in (2, 1, 3, 0) for b in (0, 1) if a or b]
        peers = [
            lax.rem(me // PAIR + a, RING) * PAIR + lax.rem(me + b, PAIR) for a, b in steps
        ]
    else:
        steps = []
        peers = [lax.rem(me + d, n) for d in range(1, n)]

    def scatter(part, outgoing, landing, passing, sems, rows):
        copies = {}
        order = sorted(range(n - 1), key=lambda k: relayed and steps[k] != (2, 1))
        for k in order:
            encode(piece(part, peers[k], rows), outgoing.at[k])
            if relayed and steps[k] == (2, 1):
                near = peers[steps.index((3, 1))]
                copies["first"] = send(outgoing.at[k], passing, sems, n - 1, near)
            else:
                copies[k] = send(outgoing.at[k], landing.at[k], sems, k, peers[k])
        return copies

    def pass_on(copies, landing, passing, sems):
        if relayed:
            copies.pop("first").wait()
            k = steps.index((2, 1))
            copies[k] = send(passing, landing.at[k], sems, k, peers[steps.index((3, 0))])

    def collect(copies, part, landing, rows):
        total = piece(part, me, rows)
        for k in copies:
            copies[k].wait()
            total = total + decode(landing.at[k], rows)
        return total

    def gather(total, gathered, sems):
        encode(total, gathered.at[me])
        return {
            k: send(gathered.at[me], gathered.at[me], sems, k, peers[k])
            for k in range(n - 1)
            if not (relayed and steps[k][0] == 2)
        }

    def hand_on(copies, gathered, sems):
        if relayed:
            for b, ahead in ((0, 1), (1, 3)):
                copies[steps.index((ahead, b))].wait_recv()
                behind = lax.rem(me // PAIR + RING - ahead, RING) * PAIR + lax.rem(me + b, PAIR)
                k = steps.index((2, b))
                peer = peers[steps.index((ahead, 0))]
                copies[k] = send(gathered.at[behind], gathered.at[behind], sems, k, peer)

    def finish(copies):
        for k in copies:
            if relayed and steps[k] in ((1, 0), (3, 1)):
                copies[k].wait_send()
            else:
                copies[k].wait()

    pl.semaphore_wait(barrier, n + 1)
    coupled_rows = len(where) * width // n
    coupled_sems = [(coupled_send.at[i], coupled_recv.at[i]) for i in range(2)]
    coupled_copies = scatter(
        coupled_part, coupled_out, coupled_in, coupled_pass, coupled_sems[0], coupled_rows
    )
    slots_copy = pltpu.make_async_remote_copy(
        src_ref=right_ref,
        dst_ref=slots_vmem,
        send_sem=slot_sem.at[0],
        recv_sem=slot_sem.at[1],
        device_id=(after, me),
        device_id_type=MESH,
    )
    slots_copy.start()

    share = LANES // n
    pairs = panels // 2
    inner_rows = halves * 2 * share
    inner_sems = [
        [(inner_send.at[i, h], inner_recv.at[i, h]) for h in range(max(pairs, halves))]
        for i in range(2)
    ]
    inner_copies = []
    for q in range(pairs):
        columns = slice(2 * q * width, 2 * (q + 1) * width)

        def project(r, total):
            span = pl.ds(r * PROJECT_SPAN, PROJECT_SPAN)
            rows = PROJECT_SPAN * BLOCK
            both = (
                v_high[span, :, columns].reshape(rows, 2 * width),
                v_low[span, :, columns].reshape(rows, 2 * width),
            )
            if q == 0:
                for i in range(PROJECT_SPAN):
                    load(x_hbm, x_buf, x_sem, r * PROJECT_SPAN + i).wait()
                high, low = split(x_buf[span].reshape(rows, eig))
                x_turned[r, :eig, :] = high.T
                x_turned[r, eig:, :] = low.T
                turned = (x_turned[r, :eig, :], x_turned[r, eig:, :])
                return total + contract(turned, both, PLAIN)
            fine = multiply(x_turned[r], both[0], PLAIN)
            crossed = multiply(x_turned[r, :eig, :], both[1], PLAIN)
            return total + (fine[:eig] + (fine[eig:] + crossed))

        projected = lax.fori_loop(
            0, blocks // PROJECT_SPAN, project, jnp.zeros((eig, 2 * width), F32)
        )
        for d in range(n):
            for h in range(halves):
                for k in range(2):
                    source = h * LANES + d * share
                    target = (d * halves + h) * 2 * share + k * share
                    inner_part[q, target : target + share, :] = projected[
                        source : source + share, k * width : (k + 1) * width
                    ]
        inner_copies.append(
            scatter(
                inner_part.at[q],
                inner_out.at[q],
                inner_in.at[q],
                inner_pass.at[q],
                inner_sems[0][q],
                inner_rows,
            )
        )
        if q == 0:
            pass_on(coupled_copies, coupled_in, coupled_pass, coupled_sems[0])
        else:
            pass_on(inner_copies[q - 1], inner_in.at[q - 1], inner_pass.at[q - 1], inner_sems[0][q - 1])
    coupled_copies = gather(
        collect(coupled_copies, coupled_part, coupled_in, coupled_rows), coupled_all, coupled_sems[1]
    )
    pass_on(inner_copies[-1], inner_in.at[pairs - 1], inner_pass.at[pairs - 1], inner_sems[0][pairs - 1])

    slots_copy.wait()
    to_smem = pltpu.make_async_copy(slots_vmem, slots_smem, slot_sem.at[2])
    to_smem.start()

    def transfer_matrix():
        f_copy.wait()
        for k in reversed(range(panels)):
            here = slice(k * width, (k + 1) * width)
            t_ref[here, here] = f_ref[k]
            if k:
                t_ref[here, : k * width] = jnp.zeros((width, k * width), F32)
            if k < panels - 1:
                later = slice((k + 1) * width, panels * width)
                row = jnp.concatenate(
                    [coupled[where[(k, j)] : where[(k, j)] + width, :] for j in range(k + 1, panels)],
                    axis=1,
                )
                inner = contract(split(row), split(t_ref[later, later]), PLAIN)
                t_ref[here, later] = -contract(split(f_ref[k]), split(inner), PLAIN)

    def update(h):
        for j in range(n):
            value = decode(inner_all.at[h, j], panels * share)
            for k in range(panels):
                inner[h, j * share : (j + 1) * share, k * width : (k + 1) * width] = value[
                    k * share : (k + 1) * share, :
                ]
        high, low = split(contract(split(t_ref[...]), split(inner[h]), COLUMNS))
        u_high[:, h * LANES : (h + 1) * LANES] = high
        u_low[:, h * LANES : (h + 1) * LANES] = low

    def finished(slot, columns):
        change = contract(
            (v_high[slot], v_low[slot]), (u_high[:, columns], u_low[:, columns]), PLAIN
        )
        value = x_buf[slot, :, columns] - change
        live = lax.broadcasted_iota(jnp.int32, value.shape, 0) < channels_ref[0, slot]
        return jnp.where(live, value, 0.0)

    kets = {}

    def right_blocks(h):
        for t in range(tile_slots):
            ket_out[h, t] = finished(slots_smem[0, t], slice(h * LANES, (h + 1) * LANES)).astype(BF16)
            copy = pltpu.make_async_remote_copy(
                src_ref=ket_out.at[h, t],
                dst_ref=ket_in.at[h, t],
                send_sem=ket_send.at[h, t],
                recv_sem=ket_recv.at[h, t],
                device_id=(before, me),
                device_id_type=MESH,
            )
            copy.start()
            kets[(h, t)] = copy

    def left_blocks():
        for t in range(tile_slots):
            occupied = occupied_ref[0, t].astype(F32)
            bras[t] = (finished(left_ref[0, t], slice(0, eig)) * occupied).astype(BF16)

    totals = [
        collect(inner_copies[q], inner_part.at[q], inner_in.at[q], inner_rows) for q in range(pairs)
    ]
    inner_copies = [
        gather(
            jnp.concatenate(
                [total[h * 2 * share : (h + 1) * 2 * share, :] for total in totals], axis=0
            ),
            inner_all.at[h],
            inner_sems[1][h],
        )
        for h in range(halves)
    ]
    hand_on(coupled_copies, coupled_all, coupled_sems[1])
    for h in range(halves):
        hand_on(inner_copies[h], inner_all.at[h], inner_sems[1][h])
    finish(coupled_copies)
    for j in range(n):
        coupled[j * coupled_rows : (j + 1) * coupled_rows, :] = decode(coupled_all.at[j], coupled_rows)
    transfer_matrix()
    to_smem.wait()
    for h in range(halves):
        finish(inner_copies[h])
        update(h)
        right_blocks(h)
    left_blocks()

    own_rows = eig // n
    tiles_copy.wait()
    sends = []
    for h in range(halves):
        total = jnp.zeros((eig, LANES), F32)
        for t in range(tile_slots):
            kets[(h, t)].wait()
            product = jnp.dot(tiles_ref[t], ket_in[h, t], preferred_element_type=F32).astype(BF16)
            total = total + lax.dot_general(
                bras[t], product, (ROWS, ((), ())), preferred_element_type=F32
            )
        own[h] = total.reshape(n, own_rows, LANES)
        dipole_out[h] = total.reshape(n, own_rows, LANES).astype(BF16)
        for d in range(1, n):
            target = lax.rem(me + d, n)
            copy = pltpu.make_async_remote_copy(
                src_ref=dipole_out.at[h, target],
                dst_ref=dipole_in.at[h, d - 1],
                send_sem=dipole_send.at[h, d - 1],
                recv_sem=dipole_recv.at[h, d - 1],
                device_id=(sym, target),
                device_id_type=MESH,
            )
            copy.start()
            sends.append((h, d, copy))
    results = [own[h, me] for h in range(halves)]
    for h, d, copy in sends:
        copy.wait()
        results[h] = results[h] + dipole_in[h, d - 1].astype(F32)
    for h in range(halves):
        out_ref[0, :, h * LANES : (h + 1) * LANES] = results[h]


def on_device(
    n,
    syms,
    vectors,
    reflectors,
    factors,
    tiles,
    tile_left,
    tile_right,
    tile_occupied_mask,
    channels,
):
    start = vectors[0]
    panels = reflectors[0]
    rows, eig = start.shape
    count, width, _ = factors.shape[1:]
    tile_slots = tiles.shape[1]
    halves = eig // LANES
    blocks = rows // BLOCK
    coupled = count * (count - 1) // 2 * width
    coupled_piece = padded(coupled // n) + PACK
    products = len(couplings(count)) * (count // 2) ** 2 * width
    scatter_piece = padded(2 * eig // n) + PACK
    inner_piece = padded(count * LANES // n) + PACK
    spans = blocks // PROJECT_SPAN
    share = eig // n
    dma = pltpu.SemaphoreType.DMA
    vmem = pl.BlockSpec(memory_space=pltpu.VMEM)
    smem = pl.BlockSpec(memory_space=pltpu.SMEM)
    hbm = pl.BlockSpec(memory_space=pl.ANY)
    return pl.pallas_call(
        functools.partial(kernel, n, syms),
        out_shape=jax.ShapeDtypeStruct((1, share, eig), F32),
        in_specs=[hbm, hbm, hbm, hbm, vmem, smem, smem, smem],
        out_specs=vmem,
        scratch_shapes=[
            pltpu.VMEM((blocks, BLOCK, eig), F32),
            pltpu.VMEM((blocks, BLOCK, count * width), F32),
            pltpu.VMEM((blocks, BLOCK, count * width), BF16),
            pltpu.VMEM((blocks, BLOCK, count * width), BF16),
            pltpu.VMEM((1, tile_slots), jnp.int32),
            pltpu.SMEM((1, tile_slots), jnp.int32),
            pltpu.VMEM((products, LANES), F32),
            pltpu.VMEM((n - 1, coupled_piece, LANES), I16),
            pltpu.VMEM((n - 1, coupled_piece, LANES), I16),
            pltpu.VMEM((coupled_piece, LANES), I16),
            pltpu.VMEM((n, coupled_piece, LANES), I16),
            pltpu.VMEM((coupled, LANES), F32),
            pltpu.VMEM((count // 2, 2 * eig, LANES), F32),
            pltpu.VMEM((count // 2, n - 1, scatter_piece, LANES), I16),
            pltpu.VMEM((count // 2, n - 1, scatter_piece, LANES), I16),
            pltpu.VMEM((count // 2, scatter_piece, LANES), I16),
            pltpu.VMEM((halves, n, inner_piece, LANES), I16),
            pltpu.VMEM((halves, LANES, count * width), F32),
            pltpu.VMEM((spans, 2 * eig, rows // spans), BF16),
            pltpu.VMEM((count * width, count * width), F32),
            pltpu.VMEM((count * width, eig), BF16),
            pltpu.VMEM((count * width, eig), BF16),
            pltpu.VMEM((halves, tile_slots, BLOCK, LANES), BF16),
            pltpu.VMEM((halves, tile_slots, BLOCK, LANES), BF16),
            pltpu.VMEM((tile_slots, BLOCK, eig), BF16),
            pltpu.VMEM((halves, n, share, LANES), F32),
            pltpu.VMEM((halves, n, share, LANES), BF16),
            pltpu.VMEM((halves, n - 1, share, LANES), BF16),
            pltpu.VMEM((count, width, width), F32),
            pltpu.VMEM((tile_slots, BLOCK, BLOCK), BF16),
            dma((blocks,)),
            dma((blocks,)),
            dma((3,)),
            dma((2,)),
            dma((2, n)),
            dma((2, n)),
            dma((2, max(halves, count // 2), n)),
            dma((2, max(halves, count // 2), n)),
            dma((halves, tile_slots)),
            dma((halves, tile_slots)),
            dma((halves, n - 1)),
            dma((halves, n - 1)),
        ],
        compiler_params=pltpu.CompilerParams(
            collective_id=0, has_side_effects=True, vmem_limit_bytes=60 * 1024 * 1024
        ),
    )(
        start.reshape(blocks, BLOCK, eig),
        panels.reshape(blocks, BLOCK, count * width),
        factors[0],
        tiles[0],
        tile_right,
        tile_left,
        tile_occupied_mask,
        channels,
    )


def solution(mesh):
    return jax.shard_map(
        functools.partial(on_device, mesh.shape["row"], mesh.shape["sym"]),
        mesh=mesh,
        in_specs=(
            P("sym", "row", None),
            P("sym", "row", None),
            P("sym", None, None, None),
            P("sym", "row", None, None),
            P("sym", "row"),
            P("sym", "row"),
            P("sym", "row"),
            P("sym", "row"),
        ),
        out_specs=P("sym", "row", None),
        check_vma=False,
    )
```

```python
import functools

import jax
import jax.numpy as jnp
from jax import lax
from jax.experimental import pallas as pl
from jax.experimental.pallas import tpu as pltpu
from jax.sharding import PartitionSpec as P

BLOCK = 512
LANES = 128
COUPLE_SPAN = 2
PROJECT_SPAN = 4
RING = 4
PAIR = 2
PACK = 16
TOP = 15.0
MARGIN = 1e-3
LEAST = 2.0**-100
MOST = 2.0**100
F32 = jnp.float32
BF16 = jnp.bfloat16
I16 = jnp.int16
MESH = pl.DeviceIdType.MESH


def split(value):
    high = value.astype(BF16)
    return high, (value - high.astype(F32)).astype(BF16)


def multiply(a, b, dims):
    return lax.dot_general(a, b, (dims, ((), ())), preferred_element_type=F32)


def contract(first, second, dims):
    high, low = first
    other_high, other_low = second
    crossed = multiply(high, other_low, dims) + multiply(low, other_high, dims)
    return multiply(high, other_high, dims) + crossed


ROWS = ((0,), (0,))
PLAIN = ((1,), (0,))
COLUMNS = ((1,), (1,))


def couplings(panels):
    levels = []
    size = panels
    while size > 1:
        starts = range(0, panels, size)
        first = [a + i for a in starts for i in range(size // 2)]
        levels.append((first, [a + size // 2 for a in first], size // 2))
        size //= 2
    return levels


def padded(rows):
    return -(-rows // PACK) * PACK


def encode(value, target):
    rows = value.shape[0]
    groups = value.reshape(rows // 8, 8, LANES)
    peak = jnp.clip(jnp.max(jnp.abs(groups), axis=0), LEAST, MOST)
    level = jnp.ceil(jnp.log2(peak) + MARGIN) - TOP
    codes = jnp.round(groups * jnp.exp2(-level)[None])
    target[:rows, :] = codes.reshape(rows, LANES).astype(jnp.int32).astype(I16)
    both = jnp.concatenate([level, level], axis=0)
    target[padded(rows) :, :] = both.astype(jnp.int32).astype(I16)


def decode(source, rows):
    level = source[padded(rows) :, :].astype(jnp.int32).astype(F32)[:8]
    groups = source[:rows, :].astype(jnp.int32).astype(F32).reshape(rows // 8, 8, LANES)
    return (groups * jnp.exp2(level)[None]).reshape(rows, LANES)


def kernel(
    n,
    syms,
    x_hbm,
    v_hbm,
    f_hbm,
    tiles_hbm,
    right_ref,
    left_ref,
    occupied_ref,
    channels_ref,
    out_ref,
    x_buf,
    v_buf,
    v_high,
    v_low,
    slots_vmem,
    slots_smem,
    coupled_part,
    coupled_out,
    coupled_in,
    coupled_all,
    coupled,
    inner_part,
    inner_out,
    inner_in,
    inner_all,
    inner,
    x_turned,
    t_ref,
    w_high,
    w_low,
    u_high,
    u_low,
    ket_out,
    ket_in,
    bras,
    own,
    dipole_out,
    dipole_in,
    f_ref,
    tiles_ref,
    x_sem,
    v_sem,
    slot_sem,
    operand_sem,
    coupled_send,
    coupled_recv,
    inner_send,
    inner_recv,
    ket_send,
    ket_recv,
    dipole_send,
    dipole_recv,
):
    panels, width, _ = f_ref.shape
    blocks, _, eig = x_buf.shape
    tile_slots = tiles_ref.shape[0]
    halves = eig // LANES
    sym = lax.axis_index("sym")
    me = lax.axis_index("row")
    after = lax.rem(sym + 1, syms)
    before = lax.rem(sym + syms - 1, syms)

    def load(source, target, sems, r):
        return pltpu.make_async_copy(source.at[r], target.at[r], sems.at[r])

    for r in range(blocks):
        load(v_hbm, v_buf, v_sem, r).start()
    for r in range(blocks):
        load(x_hbm, x_buf, x_sem, r).start()

    f_copy = pltpu.make_async_copy(f_hbm, f_ref, operand_sem.at[0])
    f_copy.start()
    tiles_copy = pltpu.make_async_copy(tiles_hbm, tiles_ref, operand_sem.at[1])
    tiles_copy.start()

    barrier = pltpu.get_barrier_semaphore()
    for d in range(1, n):
        pl.semaphore_signal(
            barrier, inc=1, device_id=(sym, lax.rem(me + d, n)), device_id_type=MESH
        )
    for other in (after, before):
        pl.semaphore_signal(barrier, inc=1, device_id=(other, me), device_id_type=MESH)

    levels = couplings(panels)

    def side(ref, span, chosen):
        rows = ref[span].reshape(COUPLE_SPAN * BLOCK, panels * width)
        return jnp.concatenate([rows[:, k * width : (k + 1) * width] for k in chosen], axis=1)

    def couple(r, sums):
        for i in range(COUPLE_SPAN):
            block = r * COUPLE_SPAN + i
            load(v_hbm, v_buf, v_sem, block).wait()
            v_high[block], v_low[block] = split(v_buf[block])
        span = pl.ds(r * COUPLE_SPAN, COUPLE_SPAN)
        return tuple(
            total
            + contract(
                (side(v_high, span, first), side(v_low, span, first)),
                (side(v_high, span, second), side(v_low, span, second)),
                ROWS,
            )
            for total, (first, second, _) in zip(sums, levels)
        )

    half_width = panels // 2 * width
    sums = lax.fori_loop(
        0,
        blocks // COUPLE_SPAN,
        couple,
        tuple(jnp.zeros((half_width, half_width), F32) for _ in levels),
    )
    where = {}
    blocks_of = [
        (total, first[i], second[j], i, j, i // size == j // size)
        for total, (first, second, size) in zip(sums, levels)
        for i in range(len(first))
        for j in range(len(second))
    ]
    place = 0
    for total, a, b, i, j, needed in sorted(blocks_of, key=lambda entry: not entry[-1]):
        coupled_part[place : place + width, :] = total[
            i * width : (i + 1) * width, j * width : (j + 1) * width
        ]
        if needed:
            where[(a, b)] = place
        place = place + width

    def piece(part, owner, rows):
        return part[pl.ds(pl.multiple_of(owner * rows, 8), rows), :]

    def send(source, target, sends, recvs, d, peer):
        copy = pltpu.make_async_remote_copy(
            src_ref=source,
            dst_ref=target,
            send_sem=sends.at[d - 1],
            recv_sem=recvs.at[d - 1],
            device_id=(sym, peer),
            device_id_type=MESH,
        )
        copy.start()
        return copy

    def scatter(part, outgoing, landing, sends, recvs, rows):
        copies = []
        for d in range(1, n):
            peer = lax.rem(me + d, n)
            encode(piece(part, peer, rows), outgoing.at[d - 1])
            copies.append(send(outgoing.at[d - 1], landing.at[d - 1], sends, recvs, d, peer))
        return copies

    def collect(copies, part, landing, rows):
        total = piece(part, me, rows)
        for d in range(1, n):
            copies[d - 1].wait()
            total = total + decode(landing.at[d - 1], rows)
        return total

    ring = n == RING * PAIR
    steps = [(a, b) for a in (2, 1, 3, 0) for b in (0, 1) if a or b]

    def at(a, b):
        return lax.rem(me // PAIR + a, RING) * PAIR + lax.rem(me + b, PAIR)

    def gather(total, gathered, sends, recvs, ringed=False):
        encode(total, gathered.at[me])
        source = gathered.at[me]
        if ringed:
            return {
                (a, b): send(source, source, sends, recvs, 1 + steps.index((a, b)), at(a, b))
                for a, b in steps
                if a != 2
            }
        return {
            d: send(source, source, sends, recvs, d, lax.rem(me + d, n)) for d in range(1, n)
        }

    def hand_on(copies, gathered, sends, recvs):
        for a, b in ((1, 0), (3, 1)):
            copies[(a, b)].wait_recv()
            source = gathered.at[at(RING - a, b)]
            copies[(2, b)] = send(
                source, source, sends, recvs, 1 + steps.index((2, b)), at(a, 0)
            )

    def finish(copies):
        for key, copy in copies.items():
            if key in ((1, 0), (3, 1)):
                copy.wait_send()
            else:
                copy.wait()

    pl.semaphore_wait(barrier, n + 1)
    coupled_rows = len(where) * width // n
    coupled_copies = scatter(
        coupled_part, coupled_out, coupled_in, coupled_send.at[0], coupled_recv.at[0], coupled_rows
    )
    slots_copy = pltpu.make_async_remote_copy(
        src_ref=right_ref,
        dst_ref=slots_vmem,
        send_sem=slot_sem.at[0],
        recv_sem=slot_sem.at[1],
        device_id=(after, me),
        device_id_type=MESH,
    )
    slots_copy.start()

    share = LANES // n
    pairs = panels // 2
    inner_rows = halves * panels * share
    for q in range(pairs):
        columns = slice(2 * q * width, 2 * (q + 1) * width)

        def project(r, total):
            span = pl.ds(r * PROJECT_SPAN, PROJECT_SPAN)
            rows = PROJECT_SPAN * BLOCK
            both = (
                v_high[span, :, columns].reshape(rows, 2 * width),
                v_low[span, :, columns].reshape(rows, 2 * width),
            )
            if q == 0:
                for i in range(PROJECT_SPAN):
                    load(x_hbm, x_buf, x_sem, r * PROJECT_SPAN + i).wait()
                high, low = split(x_buf[span].reshape(rows, eig))
                x_turned[r, :eig, :] = high.T
                x_turned[r, eig:, :] = low.T
                turned = (x_turned[r, :eig, :], x_turned[r, eig:, :])
                return total + contract(turned, both, PLAIN)
            fine = multiply(x_turned[r], both[0], PLAIN)
            crossed = multiply(x_turned[r, :eig, :], both[1], PLAIN)
            return total + (fine[:eig] + (fine[eig:] + crossed))

        projected = lax.fori_loop(
            0, blocks // PROJECT_SPAN, project, jnp.zeros((eig, 2 * width), F32)
        )
        for d in range(n):
            for h in range(halves):
                for k in range(2):
                    source = h * LANES + d * share
                    target = ((d * halves + h) * panels + 2 * q + k) * share
                    inner_part[target : target + share, :] = projected[
                        source : source + share, k * width : (k + 1) * width
                    ]
    inner_copies = scatter(
        inner_part, inner_out, inner_in, inner_send.at[0], inner_recv.at[0], inner_rows
    )
    coupled_copies = gather(
        collect(coupled_copies, coupled_part, coupled_in, coupled_rows),
        coupled_all,
        coupled_send.at[1],
        coupled_recv.at[1],
        ring,
    )

    slots_copy.wait()
    to_smem = pltpu.make_async_copy(slots_vmem, slots_smem, slot_sem.at[2])
    to_smem.start()

    def transfer_matrix():
        f_copy.wait()
        for k in reversed(range(panels)):
            here = slice(k * width, (k + 1) * width)
            t_ref[here, here] = f_ref[k]
            if k:
                t_ref[here, : k * width] = jnp.zeros((width, k * width), F32)
            if k < panels - 1:
                later = slice((k + 1) * width, panels * width)
                row = jnp.concatenate(
                    [coupled[where[(k, j)] : where[(k, j)] + width, :] for j in range(k + 1, panels)],
                    axis=1,
                )
                inner = contract(split(row), split(t_ref[later, later]), PLAIN)
                t_ref[here, later] = -contract(split(f_ref[k]), split(inner), PLAIN)

    def reflect(t):
        slot = slots_smem[0, t]
        both = contract((v_high[slot], v_low[slot]), split(t_ref[...]), PLAIN)
        w_high[t], w_low[t] = split(both)

    def unpack():
        for j in range(n):
            value = decode(inner_all.at[j], inner_rows)
            for h in range(halves):
                for k in range(panels):
                    source = (h * panels + k) * share
                    target = h * LANES + j * share
                    inner[target : target + share, k * width : (k + 1) * width] = value[
                        source : source + share, :
                    ]

    def update():
        u_high[...], u_low[...] = split(contract(split(t_ref[...]), split(inner[...]), COLUMNS))

    def masked(slot, change):
        live = lax.broadcasted_iota(jnp.int32, (BLOCK, eig), 0) < channels_ref[0, slot]
        return jnp.where(live, x_buf[slot] - change, 0.0)

    kets = {}

    def right_blocks():
        for t in range(tile_slots):
            change = contract((w_high[t], w_low[t]), split(inner[...]), COLUMNS)
            value = masked(slots_smem[0, t], change).astype(BF16)
            for h in range(halves):
                ket_out[h, t] = value[:, h * LANES : (h + 1) * LANES]
                copy = pltpu.make_async_remote_copy(
                    src_ref=ket_out.at[h, t],
                    dst_ref=ket_in.at[h, t],
                    send_sem=ket_send.at[h, t],
                    recv_sem=ket_recv.at[h, t],
                    device_id=(before, me),
                    device_id_type=MESH,
                )
                copy.start()
                kets[(h, t)] = copy

    def left_blocks():
        for t in range(tile_slots):
            occupied = occupied_ref[0, t].astype(F32)
            slot = left_ref[0, t]
            change = contract((v_high[slot], v_low[slot]), (u_high[...], u_low[...]), PLAIN)
            bras[t] = (masked(slot, change) * occupied).astype(BF16)

    inner_copies = gather(
        collect(inner_copies, inner_part, inner_in, inner_rows),
        inner_all,
        inner_send.at[1],
        inner_recv.at[1],
        ring,
    )
    if ring:
        hand_on(coupled_copies, coupled_all, coupled_send.at[1], coupled_recv.at[1])
    if ring:
        hand_on(inner_copies, inner_all, inner_send.at[1], inner_recv.at[1])
    finish(coupled_copies)
    for j in range(n):
        coupled[j * coupled_rows : (j + 1) * coupled_rows, :] = decode(coupled_all.at[j], coupled_rows)
    transfer_matrix()
    to_smem.wait()
    for t in range(tile_slots):
        reflect(t)
    finish(inner_copies)
    unpack()
    right_blocks()
    update()
    left_blocks()

    own_rows = eig // n
    tiles_copy.wait()
    sends = []
    totals = [jnp.zeros((eig, LANES), F32) for _ in range(halves)]
    for t in range(tile_slots):
        for h in range(halves):
            kets[(h, t)].wait()
            product = jnp.dot(tiles_ref[t], ket_in[h, t], preferred_element_type=F32).astype(BF16)
            totals[h] = totals[h] + multiply(bras[t], product, ROWS)
            if t < tile_slots - 1:
                continue
            own[h] = totals[h].reshape(n, own_rows, LANES)
            dipole_out[h] = totals[h].reshape(n, own_rows, LANES).astype(BF16)
            for d in range(1, n):
                target = lax.rem(me + d, n)
                copy = pltpu.make_async_remote_copy(
                    src_ref=dipole_out.at[h, target],
                    dst_ref=dipole_in.at[h, d - 1],
                    send_sem=dipole_send.at[h, d - 1],
                    recv_sem=dipole_recv.at[h, d - 1],
                    device_id=(sym, target),
                    device_id_type=MESH,
                )
                copy.start()
                sends.append((h, d, copy))
    results = [own[h, me] for h in range(halves)]
    for h, d, copy in sends:
        copy.wait()
        results[h] = results[h] + dipole_in[h, d - 1].astype(F32)
    for h in range(halves):
        out_ref[0, :, h * LANES : (h + 1) * LANES] = results[h]


def on_device(
    n,
    syms,
    vectors,
    reflectors,
    factors,
    tiles,
    tile_left,
    tile_right,
    tile_occupied_mask,
    channels,
):
    start = vectors[0]
    panels = reflectors[0]
    rows, eig = start.shape
    count, width, _ = factors.shape[1:]
    tile_slots = tiles.shape[1]
    halves = eig // LANES
    blocks = rows // BLOCK
    coupled = count * (count - 1) // 2 * width
    coupled_piece = padded(coupled // n) + PACK
    products = len(couplings(count)) * (count // 2) ** 2 * width
    inner_piece = padded(count * eig // n) + PACK
    spans = blocks // PROJECT_SPAN
    share = eig // n
    dma = pltpu.SemaphoreType.DMA
    vmem = pl.BlockSpec(memory_space=pltpu.VMEM)
    smem = pl.BlockSpec(memory_space=pltpu.SMEM)
    hbm = pl.BlockSpec(memory_space=pl.ANY)
    return pl.pallas_call(
        functools.partial(kernel, n, syms),
        out_shape=jax.ShapeDtypeStruct((1, share, eig), F32),
        in_specs=[hbm, hbm, hbm, hbm, vmem, smem, smem, smem],
        out_specs=vmem,
        scratch_shapes=[
            pltpu.VMEM((blocks, BLOCK, eig), F32),
            pltpu.VMEM((blocks, BLOCK, count * width), F32),
            pltpu.VMEM((blocks, BLOCK, count * width), BF16),
            pltpu.VMEM((blocks, BLOCK, count * width), BF16),
            pltpu.VMEM((1, tile_slots), jnp.int32),
            pltpu.SMEM((1, tile_slots), jnp.int32),
            pltpu.VMEM((products, LANES), F32),
            pltpu.VMEM((n - 1, coupled_piece, LANES), I16),
            pltpu.VMEM((n - 1, coupled_piece, LANES), I16),
            pltpu.VMEM((n, coupled_piece, LANES), I16),
            pltpu.VMEM((coupled, LANES), F32),
            pltpu.VMEM((count * eig, LANES), F32),
            pltpu.VMEM((n - 1, inner_piece, LANES), I16),
            pltpu.VMEM((n - 1, inner_piece, LANES), I16),
            pltpu.VMEM((n, inner_piece, LANES), I16),
            pltpu.VMEM((eig, count * width), F32),
            pltpu.VMEM((spans, 2 * eig, rows // spans), BF16),
            pltpu.VMEM((count * width, count * width), F32),
            pltpu.VMEM((tile_slots, BLOCK, count * width), BF16),
            pltpu.VMEM((tile_slots, BLOCK, count * width), BF16),
            pltpu.VMEM((count * width, eig), BF16),
            pltpu.VMEM((count * width, eig), BF16),
            pltpu.VMEM((halves, tile_slots, BLOCK, LANES), BF16),
            pltpu.VMEM((halves, tile_slots, BLOCK, LANES), BF16),
            pltpu.VMEM((tile_slots, BLOCK, eig), BF16),
            pltpu.VMEM((halves, n, share, LANES), F32),
            pltpu.VMEM((halves, n, share, LANES), BF16),
            pltpu.VMEM((halves, n - 1, share, LANES), BF16),
            pltpu.VMEM((count, width, width), F32),
            pltpu.VMEM((tile_slots, BLOCK, BLOCK), BF16),
            dma((blocks,)),
            dma((blocks,)),
            dma((3,)),
            dma((2,)),
            dma((2, n - 1)),
            dma((2, n - 1)),
            dma((2, n - 1)),
            dma((2, n - 1)),
            dma((halves, tile_slots)),
            dma((halves, tile_slots)),
            dma((halves, n - 1)),
            dma((halves, n - 1)),
        ],
        compiler_params=pltpu.CompilerParams(
            collective_id=0, has_side_effects=True, vmem_limit_bytes=60 * 1024 * 1024
        ),
    )(
        start.reshape(blocks, BLOCK, eig),
        panels.reshape(blocks, BLOCK, count * width),
        factors[0],
        tiles[0],
        tile_right,
        tile_left,
        tile_occupied_mask,
        channels,
    )


def solution(mesh):
    return jax.shard_map(
        functools.partial(on_device, mesh.shape["row"], mesh.shape["sym"]),
        mesh=mesh,
        in_specs=(
            P("sym", "row", None),
            P("sym", "row", None),
            P("sym", None, None, None),
            P("sym", "row", None, None),
            P("sym", "row"),
            P("sym", "row"),
            P("sym", "row"),
            P("sym", "row"),
        ),
        out_specs=P("sym", "row", None),
        check_vma=False,
    )
```

```python
import functools

import jax
import jax.numpy as jnp
from jax import lax
from jax.experimental import pallas as pl
from jax.experimental.pallas import tpu as pltpu
from jax.sharding import PartitionSpec as P

BLOCK = 512
LANES = 128
COUPLE_SPAN = 2
PROJECT_SPAN = 4
RING = 4
PAIR = 2
PACK = 16
TOP = 15.0
MARGIN = 1e-3
LEAST = 2.0**-100
MOST = 2.0**100
F32 = jnp.float32
BF16 = jnp.bfloat16
I16 = jnp.int16
MESH = pl.DeviceIdType.MESH


def split(value):
    high = value.astype(BF16)
    return high, (value - high.astype(F32)).astype(BF16)


def multiply(a, b, dims):
    return lax.dot_general(a, b, (dims, ((), ())), preferred_element_type=F32)


def contract(first, second, dims):
    high, low = first
    other_high, other_low = second
    crossed = multiply(high, other_low, dims) + multiply(low, other_high, dims)
    return multiply(high, other_high, dims) + crossed


ROWS = ((0,), (0,))
PLAIN = ((1,), (0,))
COLUMNS = ((1,), (1,))


def couplings(panels):
    levels = []
    size = panels
    while size > 1:
        starts = range(0, panels, size)
        first = [a + i for a in starts for i in range(size // 2)]
        levels.append((first, [a + size // 2 for a in first], size // 2))
        size //= 2
    return levels


def padded(rows):
    return -(-rows // PACK) * PACK


def encode(value, target):
    rows = value.shape[0]
    groups = value.reshape(rows // 8, 8, LANES)
    peak = jnp.clip(jnp.max(jnp.abs(groups), axis=0), LEAST, MOST)
    level = jnp.ceil(jnp.log2(peak) + MARGIN) - TOP
    codes = jnp.round(groups * jnp.exp2(-level)[None])
    target[:rows, :] = codes.reshape(rows, LANES).astype(jnp.int32).astype(I16)
    target[padded(rows) :, :] = level.astype(jnp.int32).astype(I16)


def decode(source, rows):
    level = source[padded(rows) :, :].astype(jnp.int32).astype(F32)
    groups = source[:rows, :].astype(jnp.int32).astype(F32).reshape(rows // 8, 8, LANES)
    return (groups * jnp.exp2(level)[None]).reshape(rows, LANES)


def kernel(
    n,
    syms,
    x_hbm,
    v_hbm,
    f_hbm,
    tiles_hbm,
    right_ref,
    left_ref,
    occupied_ref,
    channels_ref,
    out_ref,
    x_buf,
    v_buf,
    v_high,
    v_low,
    slots_vmem,
    slots_smem,
    coupled_part,
    coupled_out,
    coupled_in,
    coupled_all,
    coupled,
    inner_part,
    inner_out,
    inner_in,
    inner_all,
    inner,
    x_turned,
    t_ref,
    w_high,
    w_low,
    u_high,
    u_low,
    ket_out,
    ket_in,
    bras,
    own,
    dipole_out,
    dipole_in,
    f_ref,
    tiles_ref,
    x_sem,
    v_sem,
    slot_sem,
    operand_sem,
    coupled_send,
    coupled_recv,
    inner_send,
    inner_recv,
    ket_send,
    ket_recv,
    dipole_send,
    dipole_recv,
):
    panels, width, _ = f_ref.shape
    blocks, _, eig = x_buf.shape
    tile_slots = tiles_ref.shape[0]
    halves = eig // LANES
    sym = lax.axis_index("sym")
    me = lax.axis_index("row")
    after = lax.rem(sym + 1, syms)
    before = lax.rem(sym + syms - 1, syms)

    def load(source, target, sems, r):
        return pltpu.make_async_copy(source.at[r], target.at[r], sems.at[r])

    for r in range(blocks):
        load(v_hbm, v_buf, v_sem, r).start()
    for r in range(blocks):
        load(x_hbm, x_buf, x_sem, r).start()

    f_copy = pltpu.make_async_copy(f_hbm, f_ref, operand_sem.at[0])
    f_copy.start()
    tiles_copy = pltpu.make_async_copy(tiles_hbm, tiles_ref, operand_sem.at[1])
    tiles_copy.start()

    barrier = pltpu.get_barrier_semaphore()
    for d in range(1, n):
        pl.semaphore_signal(
            barrier, inc=1, device_id=(sym, lax.rem(me + d, n)), device_id_type=MESH
        )
    for other in (after, before):
        pl.semaphore_signal(barrier, inc=1, device_id=(other, me), device_id_type=MESH)

    levels = couplings(panels)

    def side(ref, span, chosen):
        rows = ref[span].reshape(COUPLE_SPAN * BLOCK, panels * width)
        return jnp.concatenate([rows[:, k * width : (k + 1) * width] for k in chosen], axis=1)

    def couple(r, sums):
        for i in range(COUPLE_SPAN):
            block = r * COUPLE_SPAN + i
            load(v_hbm, v_buf, v_sem, block).wait()
            v_high[block], v_low[block] = split(v_buf[block])
        span = pl.ds(r * COUPLE_SPAN, COUPLE_SPAN)
        return tuple(
            total
            + contract(
                (side(v_high, span, first), side(v_low, span, first)),
                (side(v_high, span, second), side(v_low, span, second)),
                ROWS,
            )
            for total, (first, second, _) in zip(sums, levels)
        )

    half_width = panels // 2 * width
    sums = lax.fori_loop(
        0,
        blocks // COUPLE_SPAN,
        couple,
        tuple(jnp.zeros((half_width, half_width), F32) for _ in levels),
    )
    where = {}
    blocks_of = [
        (total, first[i], second[j], i, j, i // size == j // size)
        for total, (first, second, size) in zip(sums, levels)
        for i in range(len(first))
        for j in range(len(second))
    ]
    place = 0
    for total, a, b, i, j, needed in sorted(blocks_of, key=lambda entry: not entry[-1]):
        coupled_part[place : place + width, :] = total[
            i * width : (i + 1) * width, j * width : (j + 1) * width
        ]
        if needed:
            where[(a, b)] = place
        place = place + width

    def piece(part, owner, rows):
        return part[pl.ds(pl.multiple_of(owner * rows, 8), rows), :]

    def send(source, target, sends, recvs, d, peer):
        copy = pltpu.make_async_remote_copy(
            src_ref=source,
            dst_ref=target,
            send_sem=sends.at[d - 1],
            recv_sem=recvs.at[d - 1],
            device_id=(sym, peer),
            device_id_type=MESH,
        )
        copy.start()
        return copy

    def scatter(part, outgoing, landing, sends, recvs, rows):
        copies = []
        for d in range(1, n):
            peer = lax.rem(me + d, n)
            encode(piece(part, peer, rows), outgoing.at[d - 1])
            copies.append(send(outgoing.at[d - 1], landing.at[d - 1], sends, recvs, d, peer))
        return copies

    def collect(copies, part, landing, rows):
        total = piece(part, me, rows)
        for d in range(1, n):
            copies[d - 1].wait()
            total = total + decode(landing.at[d - 1], rows)
        return total

    ring = n == RING * PAIR
    steps = [(a, b) for a in (2, 1, 3, 0) for b in (0, 1) if a or b]

    def at(a, b):
        return lax.rem(me // PAIR + a, RING) * PAIR + lax.rem(me + b, PAIR)

    def gather(total, gathered, sends, recvs, ringed=False):
        encode(total, gathered.at[me])
        source = gathered.at[me]
        if ringed:
            return {
                (a, b): send(source, source, sends, recvs, 1 + steps.index((a, b)), at(a, b))
                for a, b in steps
                if a != 2
            }
        return {
            d: send(source, source, sends, recvs, d, lax.rem(me + d, n)) for d in range(1, n)
        }

    def hand_on(copies, gathered, sends, recvs):
        for a, b in ((1, 0), (3, 1)):
            copies[(a, b)].wait_recv()
            source = gathered.at[at(RING - a, b)]
            copies[(2, b)] = send(
                source, source, sends, recvs, 1 + steps.index((2, b)), at(a, 0)
            )

    def finish(copies):
        for key, copy in copies.items():
            if key in ((1, 0), (3, 1)):
                copy.wait_send()
            else:
                copy.wait()

    pl.semaphore_wait(barrier, n + 1)
    coupled_rows = len(where) * width // n
    coupled_copies = scatter(
        coupled_part, coupled_out, coupled_in, coupled_send.at[0], coupled_recv.at[0], coupled_rows
    )
    slots_copy = pltpu.make_async_remote_copy(
        src_ref=right_ref,
        dst_ref=slots_vmem,
        send_sem=slot_sem.at[0],
        recv_sem=slot_sem.at[1],
        device_id=(after, me),
        device_id_type=MESH,
    )
    slots_copy.start()

    share = LANES // n
    pairs = panels // 2
    inner_rows = halves * panels * share
    for q in range(pairs):
        columns = slice(2 * q * width, 2 * (q + 1) * width)

        def project(r, total):
            span = pl.ds(r * PROJECT_SPAN, PROJECT_SPAN)
            rows = PROJECT_SPAN * BLOCK
            both = (
                v_high[span, :, columns].reshape(rows, 2 * width),
                v_low[span, :, columns].reshape(rows, 2 * width),
            )
            if q == 0:
                for i in range(PROJECT_SPAN):
                    load(x_hbm, x_buf, x_sem, r * PROJECT_SPAN + i).wait()
                high, low = split(x_buf[span].reshape(rows, eig))
                x_turned[r, :eig, :] = high.T
                x_turned[r, eig:, :] = low.T
                turned = (x_turned[r, :eig, :], x_turned[r, eig:, :])
                return total + contract(turned, both, PLAIN)
            fine = multiply(x_turned[r], both[0], PLAIN)
            crossed = multiply(x_turned[r, :eig, :], both[1], PLAIN)
            return total + (fine[:eig] + (fine[eig:] + crossed))

        projected = lax.fori_loop(
            0, blocks // PROJECT_SPAN, project, jnp.zeros((eig, 2 * width), F32)
        )
        for d in range(n):
            for h in range(halves):
                for k in range(2):
                    source = h * LANES + d * share
                    target = ((d * halves + h) * panels + 2 * q + k) * share
                    inner_part[target : target + share, :] = projected[
                        source : source + share, k * width : (k + 1) * width
                    ]
    inner_copies = scatter(
        inner_part, inner_out, inner_in, inner_send.at[0], inner_recv.at[0], inner_rows
    )
    coupled_copies = gather(
        collect(coupled_copies, coupled_part, coupled_in, coupled_rows),
        coupled_all,
        coupled_send.at[1],
        coupled_recv.at[1],
        ring,
    )

    slots_copy.wait()
    to_smem = pltpu.make_async_copy(slots_vmem, slots_smem, slot_sem.at[2])
    to_smem.start()

    def transfer_matrix():
        f_copy.wait()
        for k in reversed(range(panels)):
            here = slice(k * width, (k + 1) * width)
            t_ref[here, here] = f_ref[k]
            if k:
                t_ref[here, : k * width] = jnp.zeros((width, k * width), F32)
            if k < panels - 1:
                later = slice((k + 1) * width, panels * width)
                row = jnp.concatenate(
                    [coupled[where[(k, j)] : where[(k, j)] + width, :] for j in range(k + 1, panels)],
                    axis=1,
                )
                inner = contract(split(row), split(t_ref[later, later]), PLAIN)
                t_ref[here, later] = -contract(split(f_ref[k]), split(inner), PLAIN)

    def reflect(t):
        slot = slots_smem[0, t]
        both = contract((v_high[slot], v_low[slot]), split(t_ref[...]), PLAIN)
        w_high[t], w_low[t] = split(both)

    def unpack():
        for j in range(n):
            value = decode(inner_all.at[j], inner_rows)
            for h in range(halves):
                for k in range(panels):
                    source = (h * panels + k) * share
                    target = h * LANES + j * share
                    inner[target : target + share, k * width : (k + 1) * width] = value[
                        source : source + share, :
                    ]

    def update():
        u_high[...], u_low[...] = split(contract(split(t_ref[...]), split(inner[...]), COLUMNS))

    def masked(slot, change):
        live = lax.broadcasted_iota(jnp.int32, (BLOCK, eig), 0) < channels_ref[0, slot]
        return jnp.where(live, x_buf[slot] - change, 0.0)

    kets = {}

    def right_blocks():
        for t in range(tile_slots):
            change = contract((w_high[t], w_low[t]), split(inner[...]), COLUMNS)
            value = masked(slots_smem[0, t], change).astype(BF16)
            for h in range(halves):
                ket_out[h, t] = value[:, h * LANES : (h + 1) * LANES]
                copy = pltpu.make_async_remote_copy(
                    src_ref=ket_out.at[h, t],
                    dst_ref=ket_in.at[h, t],
                    send_sem=ket_send.at[h, t],
                    recv_sem=ket_recv.at[h, t],
                    device_id=(before, me),
                    device_id_type=MESH,
                )
                copy.start()
                kets[(h, t)] = copy

    def left_blocks():
        for t in range(tile_slots):
            occupied = occupied_ref[0, t].astype(F32)
            slot = left_ref[0, t]
            change = contract((v_high[slot], v_low[slot]), (u_high[...], u_low[...]), PLAIN)
            bras[t] = (masked(slot, change) * occupied).astype(BF16)

    inner_copies = gather(
        collect(inner_copies, inner_part, inner_in, inner_rows),
        inner_all,
        inner_send.at[1],
        inner_recv.at[1],
        ring,
    )
    if ring:
        hand_on(coupled_copies, coupled_all, coupled_send.at[1], coupled_recv.at[1])
    if ring:
        hand_on(inner_copies, inner_all, inner_send.at[1], inner_recv.at[1])
    finish(coupled_copies)
    for j in range(n):
        coupled[j * coupled_rows : (j + 1) * coupled_rows, :] = decode(coupled_all.at[j], coupled_rows)
    transfer_matrix()
    to_smem.wait()
    for t in range(tile_slots):
        reflect(t)
    finish(inner_copies)
    unpack()
    right_blocks()
    update()
    left_blocks()

    own_rows = eig // n
    tiles_copy.wait()
    sends = []
    totals = [jnp.zeros((eig, LANES), F32) for _ in range(halves)]
    for t in range(tile_slots):
        for h in range(halves):
            kets[(h, t)].wait()
            product = jnp.dot(tiles_ref[t], ket_in[h, t], preferred_element_type=F32).astype(BF16)
            totals[h] = totals[h] + multiply(bras[t], product, ROWS)
            if t < tile_slots - 1:
                continue
            own[h] = totals[h].reshape(n, own_rows, LANES)
            dipole_out[h] = totals[h].reshape(n, own_rows, LANES).astype(BF16)
            for d in range(1, n):
                target = lax.rem(me + d, n)
                copy = pltpu.make_async_remote_copy(
                    src_ref=dipole_out.at[h, target],
                    dst_ref=dipole_in.at[h, d - 1],
                    send_sem=dipole_send.at[h, d - 1],
                    recv_sem=dipole_recv.at[h, d - 1],
                    device_id=(sym, target),
                    device_id_type=MESH,
                )
                copy.start()
                sends.append((h, d, copy))
    results = [own[h, me] for h in range(halves)]
    for h, d, copy in sends:
        copy.wait()
        results[h] = results[h] + dipole_in[h, d - 1].astype(F32)
    for h in range(halves):
        out_ref[0, :, h * LANES : (h + 1) * LANES] = results[h]


def on_device(
    n,
    syms,
    vectors,
    reflectors,
    factors,
    tiles,
    tile_left,
    tile_right,
    tile_occupied_mask,
    channels,
):
    start = vectors[0]
    panels = reflectors[0]
    rows, eig = start.shape
    count, width, _ = factors.shape[1:]
    tile_slots = tiles.shape[1]
    halves = eig // LANES
    blocks = rows // BLOCK
    coupled = count * (count - 1) // 2 * width
    coupled_piece = padded(coupled // n) + 8
    products = len(couplings(count)) * (count // 2) ** 2 * width
    inner_piece = padded(count * eig // n) + 8
    spans = blocks // PROJECT_SPAN
    share = eig // n
    dma = pltpu.SemaphoreType.DMA
    vmem = pl.BlockSpec(memory_space=pltpu.VMEM)
    smem = pl.BlockSpec(memory_space=pltpu.SMEM)
    hbm = pl.BlockSpec(memory_space=pl.ANY)
    return pl.pallas_call(
        functools.partial(kernel, n, syms),
        out_shape=jax.ShapeDtypeStruct((1, share, eig), F32),
        in_specs=[hbm, hbm, hbm, hbm, vmem, smem, smem, smem],
        out_specs=vmem,
        scratch_shapes=[
            pltpu.VMEM((blocks, BLOCK, eig), F32),
            pltpu.VMEM((blocks, BLOCK, count * width), F32),
            pltpu.VMEM((blocks, BLOCK, count * width), BF16),
            pltpu.VMEM((blocks, BLOCK, count * width), BF16),
            pltpu.VMEM((1, tile_slots), jnp.int32),
            pltpu.SMEM((1, tile_slots), jnp.int32),
            pltpu.VMEM((products, LANES), F32),
            pltpu.VMEM((n - 1, coupled_piece, LANES), I16),
            pltpu.VMEM((n - 1, coupled_piece, LANES), I16),
            pltpu.VMEM((n, coupled_piece, LANES), I16),
            pltpu.VMEM((coupled, LANES), F32),
            pltpu.VMEM((count * eig, LANES), F32),
            pltpu.VMEM((n - 1, inner_piece, LANES), I16),
            pltpu.VMEM((n - 1, inner_piece, LANES), I16),
            pltpu.VMEM((n, inner_piece, LANES), I16),
            pltpu.VMEM((eig, count * width), F32),
            pltpu.VMEM((spans, 2 * eig, rows // spans), BF16),
            pltpu.VMEM((count * width, count * width), F32),
            pltpu.VMEM((tile_slots, BLOCK, count * width), BF16),
            pltpu.VMEM((tile_slots, BLOCK, count * width), BF16),
            pltpu.VMEM((count * width, eig), BF16),
            pltpu.VMEM((count * width, eig), BF16),
            pltpu.VMEM((halves, tile_slots, BLOCK, LANES), BF16),
            pltpu.VMEM((halves, tile_slots, BLOCK, LANES), BF16),
            pltpu.VMEM((tile_slots, BLOCK, eig), BF16),
            pltpu.VMEM((halves, n, share, LANES), F32),
            pltpu.VMEM((halves, n, share, LANES), BF16),
            pltpu.VMEM((halves, n - 1, share, LANES), BF16),
            pltpu.VMEM((count, width, width), F32),
            pltpu.VMEM((tile_slots, BLOCK, BLOCK), BF16),
            dma((blocks,)),
            dma((blocks,)),
            dma((3,)),
            dma((2,)),
            dma((2, n - 1)),
            dma((2, n - 1)),
            dma((2, n - 1)),
            dma((2, n - 1)),
            dma((halves, tile_slots)),
            dma((halves, tile_slots)),
            dma((halves, n - 1)),
            dma((halves, n - 1)),
        ],
        compiler_params=pltpu.CompilerParams(
            collective_id=0, has_side_effects=True, vmem_limit_bytes=60 * 1024 * 1024
        ),
    )(
        start.reshape(blocks, BLOCK, eig),
        panels.reshape(blocks, BLOCK, count * width),
        factors[0],
        tiles[0],
        tile_right,
        tile_left,
        tile_occupied_mask,
        channels,
    )


def solution(mesh):
    return jax.shard_map(
        functools.partial(on_device, mesh.shape["row"], mesh.shape["sym"]),
        mesh=mesh,
        in_specs=(
            P("sym", "row", None),
            P("sym", "row", None),
            P("sym", None, None, None),
            P("sym", "row", None, None),
            P("sym", "row"),
            P("sym", "row"),
            P("sym", "row"),
            P("sym", "row"),
        ),
        out_specs=P("sym", "row", None),
        check_vma=False,
    )
```

```python
import functools

import jax
import jax.numpy as jnp
from jax import lax
from jax.experimental import pallas as pl
from jax.experimental.pallas import tpu as pltpu
from jax.sharding import PartitionSpec as P

BLOCK = 512
LANES = 128
COUPLE_SPAN = 2
PROJECT_SPAN = 4
RING = 4
PAIR = 2
PACK = 16
TOP = 15.0
MARGIN = 1e-3
LEAST = 2.0**-100
MOST = 2.0**100
F32 = jnp.float32
BF16 = jnp.bfloat16
I16 = jnp.int16
MESH = pl.DeviceIdType.MESH


def split(value):
    high = value.astype(BF16)
    return high, (value - high.astype(F32)).astype(BF16)


def multiply(a, b, dims):
    return lax.dot_general(a, b, (dims, ((), ())), preferred_element_type=F32)


def contract(first, second, dims):
    high, low = first
    other_high, other_low = second
    crossed = multiply(high, other_low, dims) + multiply(low, other_high, dims)
    return multiply(high, other_high, dims) + crossed


ROWS = ((0,), (0,))
PLAIN = ((1,), (0,))
COLUMNS = ((1,), (1,))


def couplings(panels):
    levels = []
    size = panels
    while size > 1:
        starts = range(0, panels, size)
        first = [a + i for a in starts for i in range(size // 2)]
        levels.append((first, [a + size // 2 for a in first], size // 2))
        size //= 2
    return levels


def padded(rows):
    return -(-rows // PACK) * PACK


def encode(value, target):
    rows = value.shape[0]
    groups = value.reshape(rows // 8, 8, LANES)
    peak = jnp.clip(jnp.max(jnp.abs(groups), axis=0), LEAST, MOST)
    level = jnp.ceil(jnp.log2(peak) + MARGIN) - TOP
    codes = jnp.round(groups * jnp.exp2(-level)[None])
    target[:rows, :] = codes.reshape(rows, LANES).astype(jnp.int32).astype(I16)
    target[padded(rows) :, :] = level.astype(jnp.int32).astype(I16)


def decode(source, rows):
    level = source[padded(rows) :, :].astype(jnp.int32).astype(F32)
    groups = source[:rows, :].astype(jnp.int32).astype(F32).reshape(rows // 8, 8, LANES)
    return (groups * jnp.exp2(level)[None]).reshape(rows, LANES)


def kernel(
    n,
    syms,
    x_hbm,
    v_hbm,
    f_hbm,
    tiles_hbm,
    right_ref,
    left_ref,
    occupied_ref,
    channels_ref,
    out_ref,
    x_buf,
    v_buf,
    v_high,
    v_low,
    slots_vmem,
    slots_smem,
    coupled_part,
    coupled_out,
    coupled_in,
    coupled_all,
    coupled,
    inner_part,
    inner_out,
    inner_in,
    inner_all,
    inner,
    x_turned,
    t_ref,
    w_high,
    w_low,
    u_high,
    u_low,
    ket_out,
    ket_in,
    bras,
    own,
    dipole_out,
    dipole_in,
    f_ref,
    tiles_ref,
    x_sem,
    v_sem,
    slot_sem,
    operand_sem,
    coupled_send,
    coupled_recv,
    inner_send,
    inner_recv,
    ket_send,
    ket_recv,
    dipole_send,
    dipole_recv,
):
    panels, width, _ = f_ref.shape
    blocks, _, eig = x_buf.shape
    tile_slots = tiles_ref.shape[0]
    halves = eig // LANES
    sym = lax.axis_index("sym")
    me = lax.axis_index("row")
    after = lax.rem(sym + 1, syms)
    before = lax.rem(sym + syms - 1, syms)

    def load(source, target, sems, r):
        return pltpu.make_async_copy(source.at[r], target.at[r], sems.at[r])

    for r in range(blocks):
        load(v_hbm, v_buf, v_sem, r).start()
    for r in range(blocks):
        load(x_hbm, x_buf, x_sem, r).start()

    f_copy = pltpu.make_async_copy(f_hbm, f_ref, operand_sem.at[0])
    f_copy.start()
    tiles_copy = pltpu.make_async_copy(tiles_hbm, tiles_ref, operand_sem.at[1])
    tiles_copy.start()

    barrier = pltpu.get_barrier_semaphore()
    for d in range(1, n):
        pl.semaphore_signal(
            barrier, inc=1, device_id=(sym, lax.rem(me + d, n)), device_id_type=MESH
        )
    for other in (after, before):
        pl.semaphore_signal(barrier, inc=1, device_id=(other, me), device_id_type=MESH)

    levels = couplings(panels)

    def side(ref, span, chosen):
        rows = ref[span].reshape(COUPLE_SPAN * BLOCK, panels * width)
        return jnp.concatenate([rows[:, k * width : (k + 1) * width] for k in chosen], axis=1)

    def couple(r, sums):
        for i in range(COUPLE_SPAN):
            block = r * COUPLE_SPAN + i
            load(v_hbm, v_buf, v_sem, block).wait()
            v_high[block], v_low[block] = split(v_buf[block])
        span = pl.ds(r * COUPLE_SPAN, COUPLE_SPAN)
        return tuple(
            total
            + contract(
                (side(v_high, span, first), side(v_low, span, first)),
                (side(v_high, span, second), side(v_low, span, second)),
                ROWS,
            )
            for total, (first, second, _) in zip(sums, levels)
        )

    half_width = panels // 2 * width
    sums = lax.fori_loop(
        0,
        blocks // COUPLE_SPAN,
        couple,
        tuple(jnp.zeros((half_width, half_width), F32) for _ in levels),
    )
    where = {}
    blocks_of = [
        (total, first[i], second[j], i, j, i // size == j // size)
        for total, (first, second, size) in zip(sums, levels)
        for i in range(len(first))
        for j in range(len(second))
    ]
    place = 0
    for total, a, b, i, j, needed in sorted(blocks_of, key=lambda entry: not entry[-1]):
        coupled_part[place : place + width, :] = total[
            i * width : (i + 1) * width, j * width : (j + 1) * width
        ]
        if needed:
            where[(a, b)] = place
        place = place + width

    def piece(part, owner, rows):
        return part[pl.ds(pl.multiple_of(owner * rows, 8), rows), :]

    def send(source, target, sends, recvs, d, peer):
        copy = pltpu.make_async_remote_copy(
            src_ref=source,
            dst_ref=target,
            send_sem=sends.at[d - 1],
            recv_sem=recvs.at[d - 1],
            device_id=(sym, peer),
            device_id_type=MESH,
        )
        copy.start()
        return copy

    def scatter(part, outgoing, landing, sends, recvs, rows):
        copies = {}
        for d in sorted(range(1, n), key=lambda d: abs(2 * d - n)):
            peer = lax.rem(me + d, n)
            encode(piece(part, peer, rows), outgoing.at[d - 1])
            copies[d] = send(outgoing.at[d - 1], landing.at[d - 1], sends, recvs, d, peer)
        return [copies[d] for d in range(1, n)]

    def collect(copies, part, landing, rows):
        total = piece(part, me, rows)
        for d in range(1, n):
            copies[d - 1].wait()
            total = total + decode(landing.at[d - 1], rows)
        return total

    ring = n == RING * PAIR
    steps = [(a, b) for a in (2, 1, 3, 0) for b in (0, 1) if a or b]

    def at(a, b):
        return lax.rem(me // PAIR + a, RING) * PAIR + lax.rem(me + b, PAIR)

    def gather(total, gathered, sends, recvs, ringed=False):
        encode(total, gathered.at[me])
        source = gathered.at[me]
        if ringed:
            return {
                (a, b): send(source, source, sends, recvs, 1 + steps.index((a, b)), at(a, b))
                for a, b in steps
                if a != 2
            }
        return {
            d: send(source, source, sends, recvs, d, lax.rem(me + d, n)) for d in range(1, n)
        }

    def hand_on(copies, gathered, sends, recvs):
        for a, b in ((1, 0), (3, 1)):
            copies[(a, b)].wait_recv()
            source = gathered.at[at(RING - a, b)]
            copies[(2, b)] = send(
                source, source, sends, recvs, 1 + steps.index((2, b)), at(a, 0)
            )

    def finish(copies):
        for key, copy in copies.items():
            if key in ((1, 0), (3, 1)):
                copy.wait_send()
            else:
                copy.wait()

    pl.semaphore_wait(barrier, n + 1)
    coupled_rows = len(where) * width // n
    coupled_copies = scatter(
        coupled_part, coupled_out, coupled_in, coupled_send.at[0], coupled_recv.at[0], coupled_rows
    )
    slots_copy = pltpu.make_async_remote_copy(
        src_ref=right_ref,
        dst_ref=slots_vmem,
        send_sem=slot_sem.at[0],
        recv_sem=slot_sem.at[1],
        device_id=(after, me),
        device_id_type=MESH,
    )
    slots_copy.start()

    share = LANES // n
    pairs = panels // 2
    inner_rows = halves * panels * share
    for q in range(pairs):
        columns = slice(2 * q * width, 2 * (q + 1) * width)

        def project(r, total):
            span = pl.ds(r * PROJECT_SPAN, PROJECT_SPAN)
            rows = PROJECT_SPAN * BLOCK
            both = (
                v_high[span, :, columns].reshape(rows, 2 * width),
                v_low[span, :, columns].reshape(rows, 2 * width),
            )
            if q == 0:
                for i in range(PROJECT_SPAN):
                    load(x_hbm, x_buf, x_sem, r * PROJECT_SPAN + i).wait()
                high, low = split(x_buf[span].reshape(rows, eig))
                x_turned[r, :eig, :] = high.T
                x_turned[r, eig:, :] = low.T
                turned = (x_turned[r, :eig, :], x_turned[r, eig:, :])
                return total + contract(turned, both, PLAIN)
            fine = multiply(x_turned[r], both[0], PLAIN)
            crossed = multiply(x_turned[r, :eig, :], both[1], PLAIN)
            return total + (fine[:eig] + (fine[eig:] + crossed))

        projected = lax.fori_loop(
            0, blocks // PROJECT_SPAN, project, jnp.zeros((eig, 2 * width), F32)
        )
        for d in range(n):
            for h in range(halves):
                for k in range(2):
                    source = h * LANES + d * share
                    target = ((d * halves + h) * panels + 2 * q + k) * share
                    inner_part[target : target + share, :] = projected[
                        source : source + share, k * width : (k + 1) * width
                    ]
    inner_copies = scatter(
        inner_part, inner_out, inner_in, inner_send.at[0], inner_recv.at[0], inner_rows
    )
    coupled_copies = gather(
        collect(coupled_copies, coupled_part, coupled_in, coupled_rows),
        coupled_all,
        coupled_send.at[1],
        coupled_recv.at[1],
        ring,
    )

    slots_copy.wait()
    to_smem = pltpu.make_async_copy(slots_vmem, slots_smem, slot_sem.at[2])
    to_smem.start()

    def transfer_matrix():
        f_copy.wait()
        for k in reversed(range(panels)):
            here = slice(k * width, (k + 1) * width)
            t_ref[here, here] = f_ref[k]
            if k:
                t_ref[here, : k * width] = jnp.zeros((width, k * width), F32)
            if k < panels - 1:
                later = slice((k + 1) * width, panels * width)
                row = jnp.concatenate(
                    [coupled[where[(k, j)] : where[(k, j)] + width, :] for j in range(k + 1, panels)],
                    axis=1,
                )
                inner = contract(split(row), split(t_ref[later, later]), PLAIN)
                t_ref[here, later] = -contract(split(f_ref[k]), split(inner), PLAIN)

    def reflect(t):
        slot = slots_smem[0, t]
        both = contract((v_high[slot], v_low[slot]), split(t_ref[...]), PLAIN)
        w_high[t], w_low[t] = split(both)

    def unpack():
        for j in range(n):
            value = decode(inner_all.at[j], inner_rows)
            for h in range(halves):
                for k in range(panels):
                    source = (h * panels + k) * share
                    target = h * LANES + j * share
                    inner[target : target + share, k * width : (k + 1) * width] = value[
                        source : source + share, :
                    ]

    def update():
        u_high[...], u_low[...] = split(contract(split(t_ref[...]), split(inner[...]), COLUMNS))

    def masked(slot, change):
        live = lax.broadcasted_iota(jnp.int32, (BLOCK, eig), 0) < channels_ref[0, slot]
        return jnp.where(live, x_buf[slot] - change, 0.0)

    kets = {}

    def right_blocks():
        for t in range(tile_slots):
            change = contract((w_high[t], w_low[t]), split(inner[...]), COLUMNS)
            value = masked(slots_smem[0, t], change).astype(BF16)
            for h in range(halves):
                ket_out[h, t] = value[:, h * LANES : (h + 1) * LANES]
                copy = pltpu.make_async_remote_copy(
                    src_ref=ket_out.at[h, t],
                    dst_ref=ket_in.at[h, t],
                    send_sem=ket_send.at[h, t],
                    recv_sem=ket_recv.at[h, t],
                    device_id=(before, me),
                    device_id_type=MESH,
                )
                copy.start()
                kets[(h, t)] = copy

    def left_blocks():
        for t in range(tile_slots):
            occupied = occupied_ref[0, t].astype(F32)
            slot = left_ref[0, t]
            change = contract((v_high[slot], v_low[slot]), (u_high[...], u_low[...]), PLAIN)
            bras[t] = (masked(slot, change) * occupied).astype(BF16)

    inner_copies = gather(
        collect(inner_copies, inner_part, inner_in, inner_rows),
        inner_all,
        inner_send.at[1],
        inner_recv.at[1],
        ring,
    )
    if ring:
        hand_on(coupled_copies, coupled_all, coupled_send.at[1], coupled_recv.at[1])
    if ring:
        hand_on(inner_copies, inner_all, inner_send.at[1], inner_recv.at[1])
    finish(coupled_copies)
    for j in range(n):
        coupled[j * coupled_rows : (j + 1) * coupled_rows, :] = decode(coupled_all.at[j], coupled_rows)
    transfer_matrix()
    to_smem.wait()
    for t in range(tile_slots):
        reflect(t)
    finish(inner_copies)
    unpack()
    right_blocks()
    update()
    left_blocks()

    own_rows = eig // n
    tiles_copy.wait()
    sends = []
    totals = [jnp.zeros((eig, LANES), F32) for _ in range(halves)]
    for t in range(tile_slots):
        for h in range(halves):
            kets[(h, t)].wait()
            product = jnp.dot(tiles_ref[t], ket_in[h, t], preferred_element_type=F32).astype(BF16)
            totals[h] = totals[h] + multiply(bras[t], product, ROWS)
            if t < tile_slots - 1:
                continue
            own[h] = totals[h].reshape(n, own_rows, LANES)
            dipole_out[h] = totals[h].reshape(n, own_rows, LANES).astype(BF16)
            for d in range(1, n):
                target = lax.rem(me + d, n)
                copy = pltpu.make_async_remote_copy(
                    src_ref=dipole_out.at[h, target],
                    dst_ref=dipole_in.at[h, d - 1],
                    send_sem=dipole_send.at[h, d - 1],
                    recv_sem=dipole_recv.at[h, d - 1],
                    device_id=(sym, target),
                    device_id_type=MESH,
                )
                copy.start()
                sends.append((h, d, copy))
    results = [own[h, me] for h in range(halves)]
    for h, d, copy in sends:
        copy.wait()
        results[h] = results[h] + dipole_in[h, d - 1].astype(F32)
    for h in range(halves):
        out_ref[0, :, h * LANES : (h + 1) * LANES] = results[h]


def on_device(
    n,
    syms,
    vectors,
    reflectors,
    factors,
    tiles,
    tile_left,
    tile_right,
    tile_occupied_mask,
    channels,
):
    start = vectors[0]
    panels = reflectors[0]
    rows, eig = start.shape
    count, width, _ = factors.shape[1:]
    tile_slots = tiles.shape[1]
    halves = eig // LANES
    blocks = rows // BLOCK
    coupled = count * (count - 1) // 2 * width
    coupled_piece = padded(coupled // n) + 8
    products = len(couplings(count)) * (count // 2) ** 2 * width
    inner_piece = padded(count * eig // n) + 8
    spans = blocks // PROJECT_SPAN
    share = eig // n
    dma = pltpu.SemaphoreType.DMA
    vmem = pl.BlockSpec(memory_space=pltpu.VMEM)
    smem = pl.BlockSpec(memory_space=pltpu.SMEM)
    hbm = pl.BlockSpec(memory_space=pl.ANY)
    return pl.pallas_call(
        functools.partial(kernel, n, syms),
        out_shape=jax.ShapeDtypeStruct((1, share, eig), F32),
        in_specs=[hbm, hbm, hbm, hbm, vmem, smem, smem, smem],
        out_specs=vmem,
        scratch_shapes=[
            pltpu.VMEM((blocks, BLOCK, eig), F32),
            pltpu.VMEM((blocks, BLOCK, count * width), F32),
            pltpu.VMEM((blocks, BLOCK, count * width), BF16),
            pltpu.VMEM((blocks, BLOCK, count * width), BF16),
            pltpu.VMEM((1, tile_slots), jnp.int32),
            pltpu.SMEM((1, tile_slots), jnp.int32),
            pltpu.VMEM((products, LANES), F32),
            pltpu.VMEM((n - 1, coupled_piece, LANES), I16),
            pltpu.VMEM((n - 1, coupled_piece, LANES), I16),
            pltpu.VMEM((n, coupled_piece, LANES), I16),
            pltpu.VMEM((coupled, LANES), F32),
            pltpu.VMEM((count * eig, LANES), F32),
            pltpu.VMEM((n - 1, inner_piece, LANES), I16),
            pltpu.VMEM((n - 1, inner_piece, LANES), I16),
            pltpu.VMEM((n, inner_piece, LANES), I16),
            pltpu.VMEM((eig, count * width), F32),
            pltpu.VMEM((spans, 2 * eig, rows // spans), BF16),
            pltpu.VMEM((count * width, count * width), F32),
            pltpu.VMEM((tile_slots, BLOCK, count * width), BF16),
            pltpu.VMEM((tile_slots, BLOCK, count * width), BF16),
            pltpu.VMEM((count * width, eig), BF16),
            pltpu.VMEM((count * width, eig), BF16),
            pltpu.VMEM((halves, tile_slots, BLOCK, LANES), BF16),
            pltpu.VMEM((halves, tile_slots, BLOCK, LANES), BF16),
            pltpu.VMEM((tile_slots, BLOCK, eig), BF16),
            pltpu.VMEM((halves, n, share, LANES), F32),
            pltpu.VMEM((halves, n, share, LANES), BF16),
            pltpu.VMEM((halves, n - 1, share, LANES), BF16),
            pltpu.VMEM((count, width, width), F32),
            pltpu.VMEM((tile_slots, BLOCK, BLOCK), BF16),
            dma((blocks,)),
            dma((blocks,)),
            dma((3,)),
            dma((2,)),
            dma((2, n - 1)),
            dma((2, n - 1)),
            dma((2, n - 1)),
            dma((2, n - 1)),
            dma((halves, tile_slots)),
            dma((halves, tile_slots)),
            dma((halves, n - 1)),
            dma((halves, n - 1)),
        ],
        compiler_params=pltpu.CompilerParams(
            collective_id=0, has_side_effects=True, vmem_limit_bytes=60 * 1024 * 1024
        ),
    )(
        start.reshape(blocks, BLOCK, eig),
        panels.reshape(blocks, BLOCK, count * width),
        factors[0],
        tiles[0],
        tile_right,
        tile_left,
        tile_occupied_mask,
        channels,
    )


def solution(mesh):
    return jax.shard_map(
        functools.partial(on_device, mesh.shape["row"], mesh.shape["sym"]),
        mesh=mesh,
        in_specs=(
            P("sym", "row", None),
            P("sym", "row", None),
            P("sym", None, None, None),
            P("sym", "row", None, None),
            P("sym", "row"),
            P("sym", "row"),
            P("sym", "row"),
            P("sym", "row"),
        ),
        out_specs=P("sym", "row", None),
        check_vma=False,
    )
```
